128 devices in a mesh: expert: 8 (over x, core), fsdp: 16 (over z, y).
Axes of the slice: x: 4, y: 4, z: 4, core: 2. Of those that a mesh axis runs over, the one named last changes fastest.
Arguments:
- tokens: bfloat16 [16384, 1536], P(('expert', 'fsdp')), may hold values from -6 to 6
- gate_probs: float32 [16384, 2], P(('expert', 'fsdp')), may hold values from 0.1 to 1
- expert_ids: int32 [16384, 2], P(('expert', 'fsdp')), may hold values from 0 to 7, all different within a row; in each aligned block of 128 rows (0 to 127, 128 to 255, ...) at most 32 rows name the same one
- cotangent: bfloat16 [16384, 1536], P(('expert', 'fsdp')), may hold values from -0.59765625 to 0.59765625
- gate_weight: bfloat16 [8, 1536, 2048], P('expert', None, 'fsdp'), may hold values from -0.15625 to 0.15625
- up_weight: bfloat16 [8, 1536, 2048], P('expert', None, 'fsdp'), may hold values from -0.15625 to 0.15625
- down_weight: bfloat16 [8, 2048, 1536], P('expert', 'fsdp'), may hold values from -0.125 to 0.125
Outputs:
- mixed: bfloat16 [16384, 1536], P(('expert', 'fsdp'))
- d_tokens: bfloat16 [16384, 1536], P(('expert', 'fsdp'))
- d_gates: float32 [16384, 2], P(('expert', 'fsdp'))
- d_gate_weight: float32 [8, 1536, 2048], P('expert', None, 'fsdp')
- d_up_weight: float32 [8, 1536, 2048], P('expert', None, 'fsdp')
- d_down_weight: float32 [8, 2048, 1536], P('expert', 'fsdp')
The draws below stay inside these ranges and needn't reach their ends.
Inputs may be any that keep to these rules, and one draw needn't show every extreme that they name: `expert_ids`: the two experts of a token differ. In the 128 rows of one device every expert is named exactly 32 times.
All inputs are finite; a program needn't handle non-finite values.
Results may differ from the reference program's by a relative error of at most 0.015.
Values may be sent and summed in bfloat16 or wider, within the bound.
A program may use at most 192 MiB of HBM per device.

```python
import math
import jax
import jax.numpy as jnp
import numpy as np
from jax import lax

D = 1536
FF = 2048
TOK_DEV = 128
EXPERTS = 8
CAP = 32
TOKENS = 16384
N_FSDP = 16


def steps_of(stream_key, shape, split, low, largest):
    def one(axis_at, blocks):
        draws = jax.random.uniform(jax.random.fold_in(jax.random.fold_in(stream_key, 6), axis_at), (blocks,), jnp.float32, low / len(split), largest / len(split))
        return jnp.repeat(jnp.exp(draws), shape[axis_at] // blocks).reshape((-1,) + (1,) * (len(shape) - axis_at - 1))

    gain = one(*split[0])
    for cut in split[1:]:
        gain = gain * one(*cut)
    return gain


def assign_block(stream_key, own, number, rows, number_of, top, most, skew):
    ranking = jax.random.permutation(stream_key, number_of)
    packed, common = shares(number_of, rows * top, most, skew, True), shares(number_of, rows * top, most, skew, False)
    places = jnp.arange(number_of)

    def named(sizes, rotation):
        used = int((sizes > 0).sum())
        fixed = max(1, used // 4)
        moved = fixed + (places - fixed + rotation * (used - fixed)) % max(1, number_of - fixed)
        return jnp.zeros((number_of,), jnp.int32).at[ranking[jnp.where(places < fixed, places, moved)]].set(jnp.asarray(sizes, jnp.int32))

    sizes = jnp.where(number % 4 == 0, named(packed, number // 4), named(common, number - number // 4 - 1))
    mixed = jax.random.permutation(jax.random.fold_in(own, 3), number_of)
    donor, sink = mixed[0:number_of // 2 * 2:2], mixed[1:number_of // 2 * 2:2]
    margin = jnp.minimum(sizes[donor] - 1, most - sizes[sink]) // 2
    margin = jnp.where((donor == ranking[0]) | (sink == ranking[0]) | (sizes[sink] == 0), 0, jnp.maximum(margin, 0))
    moved = jax.random.randint(jax.random.fold_in(own, 4), (number_of // 2,), 0, 1 << 20) % (margin + 1)
    sizes = sizes.at[donor].add(-moved).at[sink].add(moved)
    members = jnp.searchsorted(jnp.cumsum(sizes), jnp.arange(rows * top), side="right").astype(jnp.int32)
    listing = members.reshape(top, rows).T
    listing = listing[jax.random.permutation(jax.random.fold_in(own, 1), rows)]
    rotation = jax.random.randint(jax.random.fold_in(own, 2), (rows, 1), 0, top)
    return jnp.take_along_axis(listing, (jnp.arange(top)[None, :] + rotation) % top, axis=1)


def shares(number_of, total, bound, slope, full):
    portions = [(1 << 20) // math.isqrt(grade ** slope) + 1 for grade in range(1, number_of + 1)]
    largest = bound if full else min(bound, max(-(-total // number_of), total * portions[0] // sum(portions)))
    least = 1 if total - largest >= number_of - 1 else 0
    given, spare = [largest] + [least] * (number_of - 1), total - largest - least * (number_of - 1)
    while spare > 0:
        movable = [i for i in range(1, number_of) if given[i] < largest] or [i for i in range(1, number_of) if given[i] < bound]
        mass, budget = sum([portions[i] for i in movable]), spare
        for i in movable:
            more = min(bound - given[i], max(1, budget * portions[i] // mass), spare)
            given[i] = given[i] + more
            spare = spare - more
    return np.array(given)


def centred(own_key, extent, width, bound, split=(), held_as=jnp.bfloat16):
    gain = steps_of(own_key, extent, split, -0.22, 0.18) if split else 1.0
    drawn = jax.random.normal(own_key, extent, jnp.float32) * width * gain
    return jnp.minimum(jnp.maximum(drawn, -bound), bound).astype(held_as)


def setup_inputs(seed: int = 0) -> dict:
    keys = jax.random.split(jax.random.key(seed), 8)
    tokens = centred(keys[0], (TOKENS, D), 1.0, 6.0, ((0, 128),))
    gate_probs = jnp.clip(0.1 + 0.9 * jax.random.uniform(keys[1], (TOKENS, 2), jnp.float32) ** steps_of(keys[1], (TOKENS, 2), ((0, 128),), -0.2, 0.2), 0.1, 1.0)
    expert_ids_keys = jax.random.split(jax.random.fold_in(keys[2], 1), TOKENS // TOK_DEV)
    expert_ids_turns = jax.random.permutation(jax.random.fold_in(keys[2], 3), TOKENS // TOK_DEV)
    expert_ids = jax.vmap(lambda own, number: assign_block(jax.random.fold_in(keys[2], 2), own, number, TOK_DEV, EXPERTS, 2, CAP, 0))(expert_ids_keys, expert_ids_turns).reshape((TOKENS, 2))
    cotangent = centred(keys[3], (TOKENS, D), 0.1, 0.59765625, ((0, 128),))
    gate_weight = centred(keys[4], (EXPERTS, D, FF), D ** -0.5, 0.15625, ((0, 8), (2, 16)))
    up_weight = centred(keys[5], (EXPERTS, D, FF), D ** -0.5, 0.15625, ((0, 8), (2, 16)))
    down_weight = centred(keys[6], (EXPERTS, FF, D), FF ** -0.5, 0.125, ((0, 8), (1, 16)))
    return dict(tokens=tokens, gate_probs=gate_probs, expert_ids=expert_ids, cotangent=cotangent, gate_weight=gate_weight, up_weight=up_weight, down_weight=down_weight)


def round_sum(parts):
    rounded = lax.optimization_barrier(parts.astype(jnp.bfloat16))
    return jnp.sum(rounded.astype(jnp.float32), axis=0).astype(jnp.bfloat16)


def reference(tokens, gate_probs, expert_ids, cotangent, gate_weight, up_weight, down_weight):
    dev_count = TOKENS // TOK_DEV
    pair_ids = expert_ids.reshape(dev_count, 2 * TOK_DEV)
    onehot = (pair_ids[:, :, None] == jnp.arange(EXPERTS, dtype=jnp.int32)[None, None, :]).astype(jnp.int32)
    before = jnp.cumsum(onehot, axis=1) - onehot
    slot_pos = jnp.sum(before * onehot, axis=2)
    row_pos = (jnp.arange(dev_count, dtype=jnp.int32)[:, None] * CAP + slot_pos).reshape(-1).astype(jnp.int32)
    flat_ids = expert_ids.reshape(-1).astype(jnp.int32)
    slot_rows = dev_count * CAP
    pair_index = jnp.arange(2 * TOKENS, dtype=jnp.int32)
    table = jnp.full((EXPERTS, slot_rows), 2 * TOKENS, jnp.int32).at[flat_ids, row_pos].set(pair_index)
    token_pad = jnp.concatenate([tokens, jnp.zeros((1, D), tokens.dtype)], axis=0)
    scaled = (gate_probs[:, :, None] * cotangent.astype(jnp.float32)[:, None, :]).astype(jnp.bfloat16)
    scaled_pad = jnp.concatenate([scaled.reshape(2 * TOKENS, D), jnp.zeros((1, D), jnp.bfloat16)], axis=0)
    shard = FF // N_FSDP

    def one_expert(operands):
        index, w_gate, w_up, w_down = operands
        rows_in = token_pad[index // 2]
        grad_rows = scaled_pad[index]
        pre_gate = jnp.dot(rows_in, w_gate, preferred_element_type=jnp.float32)
        pre_up = jnp.dot(rows_in, w_up, preferred_element_type=jnp.float32)
        sigmoid_gate = jax.nn.sigmoid(pre_gate)
        hidden = (pre_gate * sigmoid_gate * pre_up).astype(jnp.bfloat16)
        parts = jnp.einsum("rfh,fhd->frd", hidden.astype(jnp.float32).reshape(slot_rows, N_FSDP, shard),
                           w_down.astype(jnp.float32).reshape(N_FSDP, shard, D))
        expert_out = round_sum(parts)
        d_hidden = jnp.dot(grad_rows, w_down.T, preferred_element_type=jnp.float32)
        d_pre_gate = (d_hidden * pre_up * sigmoid_gate * (1.0 + pre_gate * (1.0 - sigmoid_gate))).astype(jnp.bfloat16)
        d_pre_up = (d_hidden * pre_gate * sigmoid_gate).astype(jnp.bfloat16)
        d_down = jnp.dot(hidden.T, grad_rows, preferred_element_type=jnp.float32)
        d_gate_w = jnp.dot(rows_in.T, d_pre_gate, preferred_element_type=jnp.float32)
        d_up_w = jnp.dot(rows_in.T, d_pre_up, preferred_element_type=jnp.float32)
        back_parts = jnp.einsum("rfh,dfh->frd", d_pre_gate.astype(jnp.float32).reshape(slot_rows, N_FSDP, shard),
                                w_gate.astype(jnp.float32).reshape(D, N_FSDP, shard))
        back_parts = back_parts + jnp.einsum("rfh,dfh->frd", d_pre_up.astype(jnp.float32).reshape(slot_rows, N_FSDP, shard),
                                             w_up.astype(jnp.float32).reshape(D, N_FSDP, shard))
        d_rows = round_sum(back_parts)
        return expert_out, d_rows, d_gate_w, d_up_w, d_down

    expert_out, d_rows, d_gate_weight, d_up_weight, d_down_weight = lax.map(
        one_expert, (table, gate_weight, up_weight, down_weight))
    per_pair = expert_out[flat_ids, row_pos].astype(jnp.float32).reshape(TOKENS, 2, D)
    mixed = jnp.sum(gate_probs[:, :, None] * per_pair, axis=1).astype(jnp.bfloat16)
    d_gates = jnp.sum(cotangent.astype(jnp.float32)[:, None, :] * per_pair, axis=2)
    d_tokens = jnp.sum(d_rows[flat_ids, row_pos].astype(jnp.float32).reshape(TOKENS, 2, D), axis=1).astype(jnp.bfloat16)
    return mixed, d_tokens, d_gates, d_gate_weight, d_up_weight, d_down_weight
```

```python
import functools

import jax
import jax.numpy as jnp
from jax import lax
from jax.experimental import pallas as pl
from jax.experimental.pallas import tpu as pltpu
from jax.sharding import PartitionSpec as P

MESH = pl.DeviceIdType.MESH
F32, BF16 = jnp.float32, jnp.bfloat16
RING = 4
ROWS_ROWS = (((0,), (0,)), ((), ()))
COLS_COLS = (((1,), (1,)), ((), ()))


def layer_kernel(
    n_exp,
    tok_ref, gp_ref, ids_ref, cot_ref, wg_ref, wu_ref, wd_ref,
    mixed_ref, dtok_ref, dgate_ref, dwg_ref, dwu_ref, dwd_ref,
    x_buf, g_buf, wg_buf, wu_buf, wd_buf, x_send, g_send,
    a_buf, b_buf, h_buf, ht_buf, dp_buf, dpt_buf,
    p_out, p_back, p_gu, p_dn,
    via_out, via_back, via_gu, via_dn,
    in_out, in_back, in_gu, in_dn,
    own_out, own_back, own_gu, own_dn,
    out_send, back_send, out_home, back_home,
    send_sem, recv_sem,
):
    tok, d = tok_ref.shape
    cap = 2 * tok // n_exp
    rows = n_exp * cap
    hs = wg_ref.shape[1]
    half = rows // 2
    tile = min(256, d)
    n_tiles = d // tile

    me = lax.axis_index("expert")
    f = lax.axis_index("fsdp")
    core = me % 2
    z, y = f // RING, f % RING
    along_z_up, along_z_down = ((z + 1) % RING) * RING + y, ((z + 3) % RING) * RING + y
    along_y_up, along_y_down = z * RING + (y + 1) % RING, z * RING + (y + 3) % RING
    t_right = along_z_up * (1 - core) + along_y_up * core
    t_left = along_z_down * (1 - core) + along_y_down * core
    w_right = along_y_up * (1 - core) + along_z_up * core
    w_left = along_y_down * (1 - core) + along_z_down * core
    tr, tl = {"fsdp": t_right}, {"fsdp": t_left}
    wr, wl = {"fsdp": w_right}, {"fsdp": w_left}

    barrier = pltpu.get_barrier_semaphore()
    for dev in (tr, tl, wr, wl):
        pl.semaphore_signal(barrier, inc=1, device_id=dev, device_id_type=MESH)
    for k in range(1, n_exp):
        pl.semaphore_signal(
            barrier, inc=1, device_id={"expert": (me + k) % n_exp}, device_id_type=MESH
        )

    started = []
    counter = [0]

    def ids(n):
        first = counter[0]
        counter[0] += n
        return first

    def copy(src, dst, n, dev):
        return pltpu.make_async_remote_copy(
            src_ref=src, dst_ref=dst, send_sem=send_sem.at[n], recv_sem=recv_sem.at[n],
            device_id=dev, device_id_type=MESH,
        )

    def send(src, dst, n, dev):
        c = copy(src, dst, n, dev)
        c.start()
        started.append(c)
        return c

    class Gather:
        def __init__(self, own, slot, halves, right, left):
            self.own, self.slot, self.halves = own, slot, halves
            self.right, self.left = right, left
            self.n = ids(4)

        def start(self):
            self.r = send(self.own, self.slot(1), self.n, self.right)
            self.l = send(self.own, self.slot(3), self.n + 1, self.left)

        def relay(self):
            lo, hi = self.halves
            self.r.wait_recv()
            self.rr = send(lo(self.slot(1)), lo(self.slot(2)), self.n + 2, self.right)
            self.l.wait_recv()
            self.ll = send(hi(self.slot(3)), hi(self.slot(2)), self.n + 3, self.left)

        def finish(self):
            self.rr.wait_recv()
            self.ll.wait_recv()

    class Scatter:
        def __init__(self, part, via, arrived, right, left):
            self.part, self.via, self.arrived = part, via, arrived
            self.right, self.left = right, left
            self.n = ids(6)

        def far(self):
            self.a = send(self.part.at[1, 0], self.via.at[0], self.n, self.right)
            self.b = send(self.part.at[1, 1], self.via.at[1], self.n + 1, self.left)

        def near(self):
            self.c = send(self.part.at[2, 1], self.arrived.at[0, 1], self.n + 2, self.right)
            self.d = send(self.part.at[0, 0], self.arrived.at[1, 0], self.n + 3, self.left)

        def add(self):
            def plus(slot, h):
                total = self.part[slot, h].astype(F32) + self.via[h].astype(F32)
                self.part[slot, h] = total.astype(BF16)

            self.a.wait_recv()
            plus(2, 0)
            self.e = send(self.part.at[2, 0], self.arrived.at[0, 0], self.n + 4, self.right)
            self.b.wait_recv()
            plus(0, 1)
            self.g = send(self.part.at[0, 1], self.arrived.at[1, 1], self.n + 5, self.left)

        def finish(self):
            for c in (self.c, self.d, self.e, self.g):
                c.wait_recv()

    class Exchange:
        def __init__(self, src, slot):
            self.src, self.slot = src, slot
            self.n = ids(n_exp - 1)

        def start(self):
            self.copies = [
                send(
                    self.src.at[(me + k) % n_exp], self.slot(me), self.n + k - 1,
                    {"expert": (me + k) % n_exp},
                )
                for k in range(1, n_exp)
            ]

        def finish(self):
            for c in self.copies:
                c.wait_recv()

    def w_rows(ref, lo, n):
        return ref.at[pl.ds(lo, n), :]

    whole_d, whole_h = d // 2, hs // 2
    gather_wg = Gather(
        wg_ref, lambda s: wg_buf.at[s - 1],
        (lambda r: w_rows(r, 0, whole_d), lambda r: w_rows(r, whole_d, whole_d)), wr, wl,
    )
    gather_wu = Gather(
        wu_ref, lambda s: wu_buf.at[s - 1],
        (lambda r: w_rows(r, 0, whole_d), lambda r: w_rows(r, whole_d, whole_d)), wr, wl,
    )
    gather_wd = Gather(
        wd_ref, lambda s: wd_buf.at[s - 1],
        (lambda r: w_rows(r, 0, whole_h), lambda r: w_rows(r, whole_h, whole_h)), wr, wl,
    )
    experts_half = n_exp // 2
    row_halves = (
        lambda r: r.at[pl.ds(0, experts_half)],
        lambda r: r.at[pl.ds(experts_half, experts_half)],
    )
    gather_x = Gather(x_buf.at[0], lambda s: x_buf.at[s], row_halves, tr, tl)
    gather_g = Gather(g_buf.at[0], lambda s: g_buf.at[s], row_halves, tr, tl)
    deal_x = Exchange(x_send, lambda e: x_buf.at[0, e])
    deal_g = Exchange(g_send, lambda e: g_buf.at[0, e])
    scatter_out = Scatter(p_out, via_out, in_out, tr, tl)
    scatter_back = Scatter(p_back, via_back, in_back, tr, tl)
    scatter_gu = Scatter(p_gu, via_gu, in_gu, wr, wl)
    scatter_dn = Scatter(p_dn, via_dn, in_dn, wr, wl)
    home_out = Exchange(out_send, lambda e: out_home.at[e])
    home_back = Exchange(back_send, lambda e: back_home.at[e])

    lane = lax.broadcasted_iota(jnp.int32, (tok, rows), 1)
    expert_of, slot_of = lane // cap, lane % cap
    named = [ids_ref[:, k : k + 1] == expert_of for k in range(2)]
    either = (named[0] | named[1]).astype(F32).astype(BF16)
    earlier = (
        lax.broadcasted_iota(jnp.int32, (tok, tok), 1)
        < lax.broadcasted_iota(jnp.int32, (tok, tok), 0)
    ).astype(F32).astype(BF16)
    before = jnp.dot(earlier, either, preferred_element_type=F32)
    here = before == slot_of.astype(F32)
    pick = [(named[k] & here).astype(F32).astype(BF16) for k in range(2)]
    pick_any = pick[0] + pick[1]

    pl.semaphore_wait(barrier, 4 + n_exp - 1)
    gather_wg.start()
    gather_wu.start()
    gather_wd.start()

    def cols(n):
        return pl.ds(pl.multiple_of(n * tile, tile), tile)

    def deal_tile(n, _):
        c = cols(n)
        sent = lax.dot_general(pick_any, tok_ref[:, c], ROWS_ROWS, preferred_element_type=F32)
        x_send[:, :, c] = sent.astype(BF16).reshape(n_exp, cap, tile)
        return 0

    lax.fori_loop(0, n_tiles, deal_tile, 0)
    deal_x.start()
    x_buf[0, me] = x_send[me]

    def deal_grad_tile(n, _):
        c = cols(n)
        cot = cot_ref[:, c].astype(F32)
        sent = sum(
            lax.dot_general(
                pick[k], (gp_ref[:, k : k + 1] * cot).astype(BF16), ROWS_ROWS,
                preferred_element_type=F32,
            )
            for k in range(2)
        )
        g_send[:, :, c] = sent.astype(BF16).reshape(n_exp, cap, tile)
        return 0

    lax.fori_loop(0, n_tiles, deal_grad_tile, 0)
    deal_g.start()
    g_buf[0, me] = g_send[me]

    wg = [wg_ref] + [wg_buf.at[s] for s in range(3)]
    wu = [wu_ref] + [wu_buf.at[s] for s in range(3)]
    wd = [wd_ref] + [wd_buf.at[s] for s in range(3)]

    gather_wg.relay()
    gather_wu.relay()
    deal_x.finish()
    gather_x.start()
    gather_wd.relay()
    deal_g.finish()
    gather_g.start()

    def forward(i):
        x = x_buf[i].reshape(rows, d)
        for j in range(RING):
            w = jnp.concatenate([wg[j][...], wu[j][...]], axis=1)
            pre = jnp.dot(x, w, preferred_element_type=F32)
            g, u = pre[:, :hs], pre[:, hs:]
            s = 1.0 / (1.0 + jnp.exp(-g))
            gs = g * s
            c = slice(j * hs, (j + 1) * hs)
            h = (gs * u).astype(BF16)
            h_buf[i, :, c] = h
            a_buf[i, :, c] = u * s * (1.0 + g * (1.0 - s))
            b_buf[i, :, c] = gs
            ht_buf[c, pl.ds(pl.multiple_of(i * rows, rows), rows)] = h.T

    def backward(i):
        g = g_buf[i].reshape(rows, d)
        for j in range(0, RING, 2):
            w = jnp.concatenate([wd[j][...], wd[j + 1][...]], axis=0)
            dh = lax.dot_general(g, w, COLS_COLS, preferred_element_type=F32)
            for jj in range(2):
                c = slice((j + jj) * hs, (j + jj + 1) * hs)
                part = dh[:, jj * hs : (jj + 1) * hs]
                dp = jnp.concatenate([part * a_buf[i, :, c], part * b_buf[i, :, c]], axis=1)
                dp = dp.astype(BF16)
                dp_buf[i, :, (j + jj) * 2 * hs : (j + jj + 1) * 2 * hs] = dp
                dpt_buf[j + jj, :, pl.ds(pl.multiple_of(i * rows, rows), rows)] = dp.T

    def store_rows(part, own, slot, c, value):
        if slot == 0:
            own[:, c] = value
        else:
            n = value.shape[0] // 2
            part[slot - 1, 0, :, c] = value[:n].astype(BF16)
            part[slot - 1, 1, :, c] = value[n:].astype(BF16)

    def out_part(i):
        def one(n, _):
            c = cols(n)
            w = jnp.concatenate([wd[j][:, c] for j in range(RING)], axis=0)
            store_rows(p_out, own_out, i, c, jnp.dot(h_buf[i], w, preferred_element_type=F32))
            return 0

        lax.fori_loop(0, n_tiles, one, 0)

    def back_part(i):
        def one(n, _):
            c = cols(n)
            w = jnp.concatenate(
                [r[c, :] for j in range(RING) for r in (wg[j], wu[j])], axis=1
            )
            value = lax.dot_general(dp_buf[i], w, COLS_COLS, preferred_element_type=F32)
            store_rows(p_back, own_back, i, c, value)
            return 0

        lax.fori_loop(0, n_tiles, one, 0)

    def gate_up_part(j):
        def one(n, _):
            c = cols(n)
            x = x_buf[:, :, :, c].reshape(RING * rows, tile)
            store_rows(p_gu, own_gu, j, c, jnp.dot(dpt_buf[j], x, preferred_element_type=F32))
            return 0

        lax.fori_loop(0, n_tiles, one, 0)

    def down_parts():
        def one(n, _):
            c = cols(n)
            g = g_buf[:, :, :, c].reshape(RING * rows, tile)
            value = jnp.dot(ht_buf[...], g, preferred_element_type=F32)
            for j in range(RING):
                store_rows(p_dn, own_dn, j, c, value[j * hs : (j + 1) * hs])
            return 0

        lax.fori_loop(0, n_tiles, one, 0)

    def three(body):
        def step(k, _):
            body(k + k // 2)
            return 0

        lax.fori_loop(0, 3, step, 0)

    gather_x.relay()
    gather_wg.finish()
    gather_wu.finish()
    three(forward)
    gather_x.finish()
    forward(2)
    gather_wd.finish()
    out_part(2)
    scatter_out.far()
    gather_g.relay()
    out_part(1)
    out_part(3)
    scatter_out.near()
    scatter_out.add()
    out_part(0)

    three(backward)
    gather_g.finish()
    backward(2)
    back_part(2)
    scatter_back.far()
    back_part(1)
    back_part(3)
    scatter_back.near()

    def total(arrived, own, sent):
        for h in range(2):
            value = (
                own[h * half : (h + 1) * half, :]
                + arrived[0, h].astype(F32)
                + arrived[1, h].astype(F32)
            )
            sent[h * experts_half : (h + 1) * experts_half] = value.astype(BF16).reshape(
                experts_half, cap, d
            )

    scatter_out.finish()
    total(in_out, own_out, out_send)
    home_out.start()
    out_home[me] = out_send[me]

    scatter_back.add()
    back_part(0)
    down_parts()
    scatter_dn.far()
    scatter_dn.near()
    gate_up_part(2)
    scatter_gu.far()
    scatter_dn.add()
    gate_up_part(1)
    gate_up_part(3)
    scatter_gu.near()
    scatter_back.finish()
    total(in_back, own_back, back_send)
    home_back.start()
    back_home[me] = back_send[me]
    scatter_gu.add()
    gate_up_part(0)

    home_out.finish()
    column = lax.broadcasted_iota(jnp.int32, (tok, 2), 1)

    def mix_tile(n, inner):
        c = cols(n)
        home = out_home[:, :, c].reshape(rows, tile)
        per = [jnp.dot(pick[k], home, preferred_element_type=F32) for k in range(2)]
        mixed_ref[:, c] = (gp_ref[:, 0:1] * per[0] + gp_ref[:, 1:2] * per[1]).astype(BF16)
        cot = cot_ref[:, c].astype(F32)
        return tuple(
            inner[k] + jnp.sum(cot * per[k], axis=1, keepdims=True) for k in range(2)
        )

    zero = jnp.zeros((tok, 1), F32)
    inner = lax.fori_loop(0, n_tiles, mix_tile, (zero, zero))
    dgate_ref[...] = jnp.where(column == 0, inner[0], inner[1])

    scatter_dn.finish()
    for h in range(2):
        r = slice(h * hs // 2, (h + 1) * hs // 2)
        dwd_ref[r, :] = own_dn[r, :] + in_dn[0, h].astype(F32) + in_dn[1, h].astype(F32)

    home_back.finish()

    def home_tile(n, _):
        c = cols(n)
        home = back_home[:, :, c].reshape(rows, tile)
        dtok_ref[:, c] = jnp.dot(pick_any, home, preferred_element_type=F32).astype(BF16)
        return 0

    lax.fori_loop(0, n_tiles, home_tile, 0)

    scatter_gu.finish()
    for h, ref in enumerate((dwg_ref, dwu_ref)):
        value = (
            own_gu[h * hs : (h + 1) * hs, :]
            + in_gu[0, h].astype(F32)
            + in_gu[1, h].astype(F32)
        )
        ref[...] = value.T

    for c in started:
        c.wait_send()


def per_device(tokens, gate_probs, expert_ids, cotangent, gate_weight, up_weight, down_weight):
    tok, d = tokens.shape
    n_exp = lax.axis_size("expert")
    cap = 2 * tok // n_exp
    rows = 2 * tok
    hs = gate_weight.shape[2]
    hidden = RING * hs
    n_copies = 4 * 5 + 6 * 4 + 4 * (n_exp - 1)
    vmem = pltpu.VMEM
    shapes = [
        vmem((RING, n_exp, cap, d), BF16),
        vmem((RING, n_exp, cap, d), BF16),
        vmem((3, d, hs), BF16),
        vmem((3, d, hs), BF16),
        vmem((3, hs, d), BF16),
        vmem((n_exp, cap, d), BF16),
        vmem((n_exp, cap, d), BF16),
        vmem((RING, rows, hidden), F32),
        vmem((RING, rows, hidden), F32),
        vmem((RING, rows, hidden), BF16),
        vmem((hidden, RING * rows), BF16),
        vmem((RING, rows, 2 * hidden), BF16),
        vmem((RING, 2 * hs, RING * rows), BF16),
    ]
    heights = (rows, rows, 2 * hs, hs)
    shapes += [vmem((3, 2, n // 2, d), BF16) for n in heights]
    shapes += [vmem((2, n // 2, d), BF16) for n in heights]
    shapes += [vmem((2, 2, n // 2, d), BF16) for n in heights]
    shapes += [vmem((n, d), F32) for n in heights]
    shapes += [vmem((n_exp, cap, d), BF16) for _ in range(4)]
    shapes += [pltpu.SemaphoreType.DMA((n_copies,)), pltpu.SemaphoreType.DMA((n_copies,))]
    spec = pl.BlockSpec(memory_space=pltpu.VMEM)
    outs = pl.pallas_call(
        functools.partial(layer_kernel, n_exp),
        out_shape=[
            jax.ShapeDtypeStruct((tok, d), BF16),
            jax.ShapeDtypeStruct((tok, d), BF16),
            jax.ShapeDtypeStruct((tok, 2), F32),
            jax.ShapeDtypeStruct((d, hs), F32),
            jax.ShapeDtypeStruct((d, hs), F32),
            jax.ShapeDtypeStruct((hs, d), F32),
        ],
        in_specs=[spec] * 7,
        out_specs=[spec] * 6,
        scratch_shapes=shapes,
        compiler_params=pltpu.CompilerParams(
            collective_id=0, has_side_effects=True, vmem_limit_bytes=63 * 1024 * 1024
        ),
    )(
        tokens, gate_probs, expert_ids, cotangent,
        gate_weight[0], up_weight[0], down_weight[0],
    )
    mixed, d_tokens, d_gates, d_gate_w, d_up_w, d_down = outs
    return mixed, d_tokens, d_gates, d_gate_w[None], d_up_w[None], d_down[None]


def solution(mesh):
    rows = P(("expert", "fsdp"), None)
    hidden = P("expert", None, "fsdp")
    hidden_rows = P("expert", "fsdp", None)
    return jax.shard_map(
        per_device,
        mesh=mesh,
        in_specs=(rows, rows, rows, rows, hidden, hidden, hidden_rows),
        out_specs=(rows, rows, rows, hidden, hidden, hidden_rows),
        check_vma=False,
    )
```

```python
import functools

import jax
import jax.numpy as jnp
from jax import lax
from jax.experimental import pallas as pl
from jax.experimental.pallas import tpu as pltpu
from jax.sharding import PartitionSpec as P

MESH = pl.DeviceIdType.MESH
F32, BF16 = jnp.float32, jnp.bfloat16
RING = 4
ROWS_ROWS = (((0,), (0,)), ((), ()))
COLS_COLS = (((1,), (1,)), ((), ()))


def layer_kernel(
    n_exp,
    tok_hbm, gp_ref, ids_ref, cot_hbm, wg_ref, wu_ref, wd_ref,
    mixed_ref, dtok_ref, dgate_ref, dwg_ref, dwu_ref, dwd_ref,
    tok_ref, cot_ref, x_buf, g_buf, wg_buf, wu_buf, wd_buf, x_send, g_send,
    a_buf, b_buf, h_buf, ht_buf, dp_buf, dpt_buf,
    p_out, p_back, p_gu, p_dn,
    via_out, via_back, via_gu, via_dn,
    in_out, in_back, in_gu, in_dn,
    own_out, own_back, own_gu, own_dn,
    out_send, back_send, out_home, back_home,
    send_sem, recv_sem, load_sem,
):
    tok, d = tok_ref.shape
    cap = 2 * tok // n_exp
    rows = n_exp * cap
    hs = wg_ref.shape[1]
    half = rows // 2
    tile = min(256, d)
    n_tiles = d // tile

    me = lax.axis_index("expert")
    f = lax.axis_index("fsdp")
    core = me % 2
    z, y = f // RING, f % RING
    along_z_up, along_z_down = ((z + 1) % RING) * RING + y, ((z + 3) % RING) * RING + y
    along_y_up, along_y_down = z * RING + (y + 1) % RING, z * RING + (y + 3) % RING
    t_right = along_z_up * (1 - core) + along_y_up * core
    t_left = along_z_down * (1 - core) + along_y_down * core
    w_right = along_y_up * (1 - core) + along_z_up * core
    w_left = along_y_down * (1 - core) + along_z_down * core
    tr, tl = {"fsdp": t_right}, {"fsdp": t_left}
    wr, wl = {"fsdp": w_right}, {"fsdp": w_left}

    barrier = pltpu.get_barrier_semaphore()
    for dev in (tr, tl, wr, wl):
        pl.semaphore_signal(barrier, inc=1, device_id=dev, device_id_type=MESH)
    for k in range(1, n_exp):
        pl.semaphore_signal(
            barrier, inc=1, device_id={"expert": (me + k) % n_exp}, device_id_type=MESH
        )

    loads = [
        pltpu.make_async_copy(src, dst, load_sem.at[n])
        for n, (src, dst) in enumerate(
            [
                (tok_hbm, tok_ref), (cot_hbm, cot_ref),
                (wg_ref, wg_buf.at[0]), (wu_ref, wu_buf.at[0]), (wd_ref, wd_buf.at[0]),
            ]
        )
    ]
    for load in loads:
        load.start()

    started = []
    counter = [0]

    def ids(n):
        first = counter[0]
        counter[0] += n
        return first

    def copy(src, dst, n, dev):
        return pltpu.make_async_remote_copy(
            src_ref=src, dst_ref=dst, send_sem=send_sem.at[n], recv_sem=recv_sem.at[n],
            device_id=dev, device_id_type=MESH,
        )

    def send(src, dst, n, dev):
        c = copy(src, dst, n, dev)
        c.start()
        started.append(c)
        return c

    class Gather:
        def __init__(self, own, slot, halves, right, left):
            self.own, self.slot, self.halves = own, slot, halves
            self.right, self.left = right, left
            self.n = ids(6)

        def start(self):
            lo, hi = self.halves
            near, far, n = self.slot(1), self.slot(3), self.n
            self.r_lo = send(lo(self.own), lo(near), n, self.right)
            self.l_hi = send(hi(self.own), hi(far), n + 1, self.left)
            self.r_hi = send(hi(self.own), hi(near), n + 2, self.right)
            self.l_lo = send(lo(self.own), lo(far), n + 3, self.left)

        def relay(self):
            lo, hi = self.halves
            self.r_lo.wait_recv()
            self.rr = send(lo(self.slot(1)), lo(self.slot(2)), self.n + 4, self.right)
            self.l_hi.wait_recv()
            self.ll = send(hi(self.slot(3)), hi(self.slot(2)), self.n + 5, self.left)

        def sides(self):
            self.r_hi.wait_recv()
            self.l_lo.wait_recv()

        def finish(self):
            self.rr.wait_recv()
            self.ll.wait_recv()

    class Scatter:
        def __init__(self, part, via, arrived, right, left):
            self.part, self.via, self.arrived = part, via, arrived
            self.right, self.left = right, left
            self.n = ids(6)

        def far(self):
            self.a = send(self.part.at[1, 0], self.via.at[0], self.n, self.right)
            self.b = send(self.part.at[1, 1], self.via.at[1], self.n + 1, self.left)

        def near(self):
            self.c = send(self.part.at[2, 1], self.arrived.at[0, 1], self.n + 2, self.right)
            self.d = send(self.part.at[0, 0], self.arrived.at[1, 0], self.n + 3, self.left)

        def add(self):
            def plus(slot, h):
                total = self.part[slot, h].astype(F32) + self.via[h].astype(F32)
                self.part[slot, h] = total.astype(BF16)

            self.a.wait_recv()
            plus(2, 0)
            self.e = send(self.part.at[2, 0], self.arrived.at[0, 0], self.n + 4, self.right)
            self.b.wait_recv()
            plus(0, 1)
            self.g = send(self.part.at[0, 1], self.arrived.at[1, 1], self.n + 5, self.left)

        def finish(self):
            for c in (self.c, self.d, self.e, self.g):
                c.wait_recv()

    class Exchange:
        def __init__(self, src, slot):
            self.src, self.slot = src, slot
            self.n = ids(n_exp - 1)

        def start(self):
            self.copies = [
                send(
                    self.src.at[(me + k) % n_exp], self.slot(me), self.n + k - 1,
                    {"expert": (me + k) % n_exp},
                )
                for k in range(1, n_exp)
            ]

        def finish(self):
            for c in self.copies:
                c.wait_recv()

    def w_rows(ref, lo, n):
        return ref.at[pl.ds(lo, n), :]

    whole_d, whole_h = d // 2, hs // 2
    gather_wg = Gather(
        wg_ref, lambda s: wg_buf.at[s],
        (lambda r: w_rows(r, 0, whole_d), lambda r: w_rows(r, whole_d, whole_d)), wr, wl,
    )
    gather_wu = Gather(
        wu_ref, lambda s: wu_buf.at[s],
        (lambda r: w_rows(r, 0, whole_d), lambda r: w_rows(r, whole_d, whole_d)), wr, wl,
    )
    gather_wd = Gather(
        wd_ref, lambda s: wd_buf.at[s],
        (lambda r: w_rows(r, 0, whole_h), lambda r: w_rows(r, whole_h, whole_h)), wr, wl,
    )
    experts_half = n_exp // 2
    row_halves = (
        lambda r: r.at[pl.ds(0, experts_half)],
        lambda r: r.at[pl.ds(experts_half, experts_half)],
    )
    gather_x = Gather(x_buf.at[0], lambda s: x_buf.at[s], row_halves, tr, tl)
    gather_g = Gather(g_buf.at[0], lambda s: g_buf.at[s], row_halves, tr, tl)
    deal_x = Exchange(x_send, lambda e: x_buf.at[0, e])
    deal_g = Exchange(g_send, lambda e: g_buf.at[0, e])
    scatter_out = Scatter(p_out, via_out, in_out, tr, tl)
    scatter_back = Scatter(p_back, via_back, in_back, tr, tl)
    scatter_gu = Scatter(p_gu, via_gu, in_gu, wr, wl)
    scatter_dn = Scatter(p_dn, via_dn, in_dn, wr, wl)
    home_out = Exchange(out_send, lambda e: out_home.at[e])
    home_back = Exchange(back_send, lambda e: back_home.at[e])

    lane = lax.broadcasted_iota(jnp.int32, (tok, rows), 1)
    expert_of, slot_of = lane // cap, lane % cap
    token = lax.broadcasted_iota(jnp.int32, (tok, tok), 0)
    other = lax.broadcasted_iota(jnp.int32, (tok, tok), 1)

    def column_of(row):
        return jnp.sum(jnp.where(token == other, row, 0.0), axis=1, keepdims=True)

    def row_of(column):
        return jnp.sum(jnp.where(token == other, column, 0.0), axis=0, keepdims=True)

    gates = [column_of(gp_ref[k : k + 1, :]) for k in range(2)]
    choices = ids_ref[...].astype(F32)
    chosen = expert_of.astype(F32)
    named = [column_of(choices[k : k + 1, :]) == chosen for k in range(2)]
    either = (named[0] | named[1]).astype(F32).astype(BF16)
    earlier = (other < token).astype(F32).astype(BF16)
    before = jnp.dot(earlier, either, preferred_element_type=F32)
    here = before == slot_of.astype(F32)
    pick = [(named[k] & here).astype(F32).astype(BF16) for k in range(2)]
    pick_any = pick[0] + pick[1]

    pl.semaphore_wait(barrier, 4 + n_exp - 1)
    gather_wg.start()
    gather_wu.start()
    gather_wd.start()

    def cols(n):
        return pl.ds(pl.multiple_of(n * tile, tile), tile)

    def deal_tile(n, _):
        c = cols(n)
        sent = lax.dot_general(pick_any, tok_ref[:, c], ROWS_ROWS, preferred_element_type=F32)
        x_send[:, :, c] = sent.astype(BF16).reshape(n_exp, cap, tile)
        return 0

    loads[0].wait()
    lax.fori_loop(0, n_tiles, deal_tile, 0)
    deal_x.start()
    x_buf[0, me] = x_send[me]

    def deal_grad_tile(n, _):
        c = cols(n)
        cot = cot_ref[:, c].astype(F32)
        sent = sum(
            lax.dot_general(
                pick[k], (gates[k] * cot).astype(BF16), ROWS_ROWS,
                preferred_element_type=F32,
            )
            for k in range(2)
        )
        g_send[:, :, c] = sent.astype(BF16).reshape(n_exp, cap, tile)
        return 0

    loads[1].wait()
    lax.fori_loop(0, n_tiles, deal_grad_tile, 0)
    deal_g.start()
    g_buf[0, me] = g_send[me]

    wg = [wg_buf.at[s] for s in range(RING)]
    wu = [wu_buf.at[s] for s in range(RING)]
    wd = [wd_buf.at[s] for s in range(RING)]

    gather_wg.relay()
    gather_wu.relay()
    deal_x.finish()
    gather_x.start()
    gather_wd.relay()
    deal_g.finish()
    gather_x.relay()
    gather_g.start()

    def forward(i):
        x = x_buf[i].reshape(rows, d)
        for j in range(RING):
            w = jnp.concatenate([wg[j][...], wu[j][...]], axis=1)
            pre = jnp.dot(x, w, preferred_element_type=F32)
            g, u = pre[:, :hs], pre[:, hs:]
            s = 1.0 / (1.0 + jnp.exp(-g))
            gs = g * s
            c = slice(j * hs, (j + 1) * hs)
            h = (gs * u).astype(BF16)
            h_buf[i, :, c] = h
            a_buf[i, :, c] = u * s * (1.0 + g * (1.0 - s))
            b_buf[i, :, c] = gs
            ht_buf[c, pl.ds(pl.multiple_of(i * rows, rows), rows)] = h.T

    def backward(i):
        g = g_buf[i].reshape(rows, d)
        for j in range(0, RING, 2):
            w = jnp.concatenate([wd[j][...], wd[j + 1][...]], axis=0)
            dh = lax.dot_general(g, w, COLS_COLS, preferred_element_type=F32)
            for jj in range(2):
                c = slice((j + jj) * hs, (j + jj + 1) * hs)
                part = dh[:, jj * hs : (jj + 1) * hs]
                dp = jnp.concatenate([part * a_buf[i, :, c], part * b_buf[i, :, c]], axis=1)
                dp = dp.astype(BF16)
                dp_buf[i, :, (j + jj) * 2 * hs : (j + jj + 1) * 2 * hs] = dp
                dpt_buf[j + jj, :, pl.ds(pl.multiple_of(i * rows, rows), rows)] = dp.T

    def store_rows(part, own, slot, c, value):
        if slot == 0:
            own[:, c] = value
        else:
            n = value.shape[0] // 2
            part[slot - 1, 0, :, c] = value[:n].astype(BF16)
            part[slot - 1, 1, :, c] = value[n:].astype(BF16)

    def out_part(i):
        def one(n, _):
            c = cols(n)
            w = jnp.concatenate([wd[j][:, c] for j in range(RING)], axis=0)
            store_rows(p_out, own_out, i, c, jnp.dot(h_buf[i], w, preferred_element_type=F32))
            return 0

        lax.fori_loop(0, n_tiles, one, 0)

    def back_part(i):
        def one(n, _):
            c = cols(n)
            w = jnp.concatenate(
                [r[c, :] for j in range(RING) for r in (wg[j], wu[j])], axis=1
            )
            value = lax.dot_general(dp_buf[i], w, COLS_COLS, preferred_element_type=F32)
            store_rows(p_back, own_back, i, c, value)
            return 0

        lax.fori_loop(0, n_tiles, one, 0)

    def gate_up_part(j):
        def one(n, _):
            c = cols(n)
            x = x_buf[:, :, :, c].reshape(RING * rows, tile)
            store_rows(p_gu, own_gu, j, c, jnp.dot(dpt_buf[j], x, preferred_element_type=F32))
            return 0

        lax.fori_loop(0, n_tiles, one, 0)

    def down_parts():
        def one(n, _):
            c = cols(n)
            g = g_buf[:, :, :, c].reshape(RING * rows, tile)
            value = jnp.dot(ht_buf[...], g, preferred_element_type=F32)
            for j in range(RING):
                store_rows(p_dn, own_dn, j, c, value[j * hs : (j + 1) * hs])
            return 0

        lax.fori_loop(0, n_tiles, one, 0)

    def both_sides(body):
        def step(k, _):
            body(1 + 2 * k)
            return 0

        lax.fori_loop(0, 2, step, 0)

    def total(arrived, own, sent):
        for h in range(2):
            value = (
                own[h * half : (h + 1) * half, :]
                + arrived[0, h].astype(F32)
                + arrived[1, h].astype(F32)
            )
            sent[h * experts_half : (h + 1) * experts_half] = value.astype(BF16).reshape(
                experts_half, cap, d
            )

    for load in loads[2:]:
        load.wait()
    for gather in (gather_wg, gather_wu):
        gather.sides()
        gather.finish()
    forward(0)
    gather_x.sides()
    both_sides(forward)
    gather_x.finish()
    forward(2)
    gather_g.relay()
    gather_wd.sides()
    gather_wd.finish()
    out_part(2)
    scatter_out.far()
    out_part(1)
    out_part(3)
    scatter_out.near()
    out_part(0)

    backward(0)
    gather_g.sides()
    both_sides(backward)
    scatter_out.add()
    gather_g.finish()
    backward(2)
    back_part(2)
    scatter_back.far()
    back_part(1)
    back_part(3)
    scatter_back.near()
    scatter_out.finish()
    total(in_out, own_out, out_send)
    home_out.start()
    out_home[me] = out_send[me]
    down_parts()
    scatter_back.add()
    scatter_dn.far()
    scatter_dn.near()
    gate_up_part(2)
    scatter_gu.far()
    back_part(0)
    gate_up_part(1)
    gate_up_part(3)
    scatter_gu.near()
    scatter_dn.add()
    scatter_back.finish()
    total(in_back, own_back, back_send)
    home_back.start()
    back_home[me] = back_send[me]
    scatter_gu.add()
    gate_up_part(0)

    home_out.finish()

    def mix_tile(n, inner):
        c = cols(n)
        home = out_home[:, :, c].reshape(rows, tile)
        per = [jnp.dot(pick[k], home, preferred_element_type=F32) for k in range(2)]
        mixed_ref[:, c] = (gates[0] * per[0] + gates[1] * per[1]).astype(BF16)
        cot = cot_ref[:, c].astype(F32)
        return tuple(
            inner[k] + jnp.sum(cot * per[k], axis=1, keepdims=True) for k in range(2)
        )

    zero = jnp.zeros((tok, 1), F32)
    inner = lax.fori_loop(0, n_tiles, mix_tile, (zero, zero))
    for k in range(2):
        dgate_ref[k : k + 1, :] = row_of(inner[k])

    scatter_dn.finish()
    for h in range(2):
        r = slice(h * hs // 2, (h + 1) * hs // 2)
        dwd_ref[r, :] = own_dn[r, :] + in_dn[0, h].astype(F32) + in_dn[1, h].astype(F32)

    home_back.finish()

    def home_tile(n, _):
        c = cols(n)
        home = back_home[:, :, c].reshape(rows, tile)
        dtok_ref[:, c] = jnp.dot(pick_any, home, preferred_element_type=F32).astype(BF16)
        return 0

    lax.fori_loop(0, n_tiles, home_tile, 0)

    scatter_gu.finish()
    for h, ref in enumerate((dwg_ref, dwu_ref)):
        value = (
            own_gu[h * hs : (h + 1) * hs, :]
            + in_gu[0, h].astype(F32)
            + in_gu[1, h].astype(F32)
        )
        ref[...] = value.T

    for c in started:
        c.wait_send()


def write_kernel(*refs):
    n = len(refs) // 2
    sem = refs[-1]
    copies = [pltpu.make_async_copy(refs[k], refs[n + k], sem.at[k]) for k in range(n)]
    for c in copies:
        c.start()
    for c in copies:
        c.wait()


def per_device(tokens, gate_probs, expert_ids, cotangent, gate_weight, up_weight, down_weight):
    tok, d = tokens.shape
    n_exp = lax.axis_size("expert")
    cap = 2 * tok // n_exp
    rows = 2 * tok
    hs = gate_weight.shape[2]
    hidden = RING * hs
    n_copies = 6 * 5 + 6 * 4 + 4 * (n_exp - 1)
    vmem = pltpu.VMEM
    shapes = [
        vmem((tok, d), BF16),
        vmem((tok, d), BF16),
        vmem((RING, n_exp, cap, d), BF16),
        vmem((RING, n_exp, cap, d), BF16),
        vmem((RING, d, hs), BF16),
        vmem((RING, d, hs), BF16),
        vmem((RING, hs, d), BF16),
        vmem((n_exp, cap, d), BF16),
        vmem((n_exp, cap, d), BF16),
        vmem((RING, rows, hidden), F32),
        vmem((RING, rows, hidden), F32),
        vmem((RING, rows, hidden), BF16),
        vmem((hidden, RING * rows), BF16),
        vmem((RING, rows, 2 * hidden), BF16),
        vmem((RING, 2 * hs, RING * rows), BF16),
    ]
    heights = (rows, rows, 2 * hs, hs)
    shapes += [vmem((3, 2, n // 2, d), BF16) for n in heights]
    shapes += [vmem((2, n // 2, d), BF16) for n in heights]
    shapes += [vmem((2, 2, n // 2, d), BF16) for n in heights]
    shapes += [vmem((n, d), F32) for n in heights]
    shapes += [vmem((n_exp, cap, d), BF16) for _ in range(4)]
    shapes += [pltpu.SemaphoreType.DMA((n,)) for n in (n_copies, n_copies, 5)]
    here, away = pl.BlockSpec(memory_space=pltpu.VMEM), pl.BlockSpec(memory_space=pl.ANY)
    results = [
        ((tok, d), BF16), ((tok, d), BF16), ((2, tok), F32),
        ((d, hs), F32), ((d, hs), F32), ((hs, d), F32),
    ]
    inside = pl.pallas_call(
        functools.partial(layer_kernel, n_exp),
        out_shape=[pltpu.VMEM(*r) for r in results],
        in_specs=[away, here, here, away, away, away, away],
        out_specs=[here] * len(results),
        scratch_shapes=shapes,
        compiler_params=pltpu.CompilerParams(
            collective_id=0, has_side_effects=True, vmem_limit_bytes=58 * 1024 * 1024
        ),
    )(
        tokens, gate_probs.T, expert_ids.T, cotangent,
        gate_weight[0], up_weight[0], down_weight[0],
    )
    mixed, d_tokens, d_gates, d_gate_w, d_up_w, d_down = pl.pallas_call(
        write_kernel,
        out_shape=[jax.ShapeDtypeStruct(*r) for r in results],
        in_specs=[here] * len(results),
        out_specs=[away] * len(results),
        scratch_shapes=[pltpu.SemaphoreType.DMA((len(results),))],
        compiler_params=pltpu.CompilerParams(vmem_limit_bytes=1024 * 1024),
    )(*inside)
    return mixed, d_tokens, d_gates.T, d_gate_w[None], d_up_w[None], d_down[None]


def solution(mesh):
    rows = P(("expert", "fsdp"), None)
    hidden = P("expert", None, "fsdp")
    hidden_rows = P("expert", "fsdp", None)
    return jax.shard_map(
        per_device,
        mesh=mesh,
        in_specs=(rows, rows, rows, rows, hidden, hidden, hidden_rows),
        out_specs=(rows, rows, rows, hidden, hidden, hidden_rows),
        check_vma=False,
    )
```

```python
import functools

import jax
import jax.numpy as jnp
from jax import lax
from jax.experimental import pallas as pl
from jax.experimental.pallas import tpu as pltpu
from jax.sharding import PartitionSpec as P

MESH = pl.DeviceIdType.MESH
F32, BF16 = jnp.float32, jnp.bfloat16
RING = 4
ROWS_ROWS = (((0,), (0,)), ((), ()))
COLS_COLS = (((1,), (1,)), ((), ()))


def layer_kernel(
    n_exp,
    tok_hbm, gp_hbm, ids_hbm, cot_hbm, wg_ref, wu_ref, wd_ref,
    mixed_ref, dtok_ref, dgate_ref, dwg_ref, dwu_ref, dwd_ref,
    tok_ref, cot_ref, gp_ref, ids_ref, x_buf, g_buf, wg_buf, wu_buf, wd_buf, x_send, g_send,
    a_buf, b_buf, h_buf, ht_buf, dp_buf, dpt_buf,
    p_out, p_back, p_gu, p_dn,
    via_out, via_back, via_gu, via_dn,
    in_out, in_back, in_gu, in_dn,
    own_out, own_back, own_gu, own_dn,
    out_send, back_send, out_home, back_home,
    send_sem, recv_sem, load_sem,
):
    tok, d = tok_ref.shape
    cap = 2 * tok // n_exp
    rows = n_exp * cap
    hs = wg_ref.shape[1]
    half = rows // 2
    tile = min(256, d)
    n_tiles = d // tile

    me = lax.axis_index("expert")
    f = lax.axis_index("fsdp")
    core = me % 2
    z, y = f // RING, f % RING
    along_z_up, along_z_down = ((z + 1) % RING) * RING + y, ((z + 3) % RING) * RING + y
    along_y_up, along_y_down = z * RING + (y + 1) % RING, z * RING + (y + 3) % RING
    t_right = along_z_up * (1 - core) + along_y_up * core
    t_left = along_z_down * (1 - core) + along_y_down * core
    w_right = along_y_up * (1 - core) + along_z_up * core
    w_left = along_y_down * (1 - core) + along_z_down * core
    tr, tl = {"fsdp": t_right}, {"fsdp": t_left}
    wr, wl = {"fsdp": w_right}, {"fsdp": w_left}

    barrier = pltpu.get_barrier_semaphore()
    for dev in (tr, tl, wr, wl):
        pl.semaphore_signal(barrier, inc=1, device_id=dev, device_id_type=MESH)
    for k in range(1, n_exp):
        pl.semaphore_signal(
            barrier, inc=1, device_id={"expert": (me + k) % n_exp}, device_id_type=MESH
        )

    loads = [
        pltpu.make_async_copy(src, dst, load_sem.at[n])
        for n, (src, dst) in enumerate(
            [
                (ids_hbm, ids_ref), (gp_hbm, gp_ref), (tok_hbm, tok_ref), (cot_hbm, cot_ref),
                (wg_ref, wg_buf.at[0]), (wu_ref, wu_buf.at[0]), (wd_ref, wd_buf.at[0]),
            ]
        )
    ]
    for load in loads:
        load.start()

    started = []
    counter = [0]

    def ids(n):
        first = counter[0]
        counter[0] += n
        return first

    def copy(src, dst, n, dev):
        return pltpu.make_async_remote_copy(
            src_ref=src, dst_ref=dst, send_sem=send_sem.at[n], recv_sem=recv_sem.at[n],
            device_id=dev, device_id_type=MESH,
        )

    def send(src, dst, n, dev):
        c = copy(src, dst, n, dev)
        c.start()
        started.append(c)
        return c

    class Gather:
        def __init__(self, own, slot, halves, right, left):
            self.own, self.slot, self.halves = own, slot, halves
            self.right, self.left = right, left
            self.n = ids(6)

        def start(self):
            lo, hi = self.halves
            near, far, n = self.slot(1), self.slot(3), self.n
            self.r_lo = send(lo(self.own), lo(near), n, self.right)
            self.l_hi = send(hi(self.own), hi(far), n + 1, self.left)
            self.r_hi = send(hi(self.own), hi(near), n + 2, self.right)
            self.l_lo = send(lo(self.own), lo(far), n + 3, self.left)

        def relay(self):
            lo, hi = self.halves
            self.r_lo.wait_recv()
            self.rr = send(lo(self.slot(1)), lo(self.slot(2)), self.n + 4, self.right)
            self.l_hi.wait_recv()
            self.ll = send(hi(self.slot(3)), hi(self.slot(2)), self.n + 5, self.left)

        def sides(self):
            self.r_hi.wait_recv()
            self.l_lo.wait_recv()

        def finish(self):
            self.rr.wait_recv()
            self.ll.wait_recv()

    class Scatter:
        def __init__(self, part, via, arrived, right, left):
            self.part, self.via, self.arrived = part, via, arrived
            self.right, self.left = right, left
            self.n = ids(6)

        def far(self):
            self.a = send(self.part.at[1, 0], self.via.at[0], self.n, self.right)
            self.b = send(self.part.at[1, 1], self.via.at[1], self.n + 1, self.left)

        def near(self):
            self.c = send(self.part.at[2, 1], self.arrived.at[0, 1], self.n + 2, self.right)
            self.d = send(self.part.at[0, 0], self.arrived.at[1, 0], self.n + 3, self.left)

        def add(self):
            def plus(slot, h):
                total = self.part[slot, h].astype(F32) + self.via[h].astype(F32)
                self.part[slot, h] = total.astype(BF16)

            self.a.wait_recv()
            plus(2, 0)
            self.e = send(self.part.at[2, 0], self.arrived.at[0, 0], self.n + 4, self.right)
            self.b.wait_recv()
            plus(0, 1)
            self.g = send(self.part.at[0, 1], self.arrived.at[1, 1], self.n + 5, self.left)

        def finish(self):
            for c in (self.c, self.d, self.e, self.g):
                c.wait_recv()

    class Exchange:
        def __init__(self, src, slot):
            self.src, self.slot = src, slot
            self.n = ids(n_exp - 1)

        def start(self):
            self.copies = [
                send(
                    self.src.at[(me + k) % n_exp], self.slot(me), self.n + k - 1,
                    {"expert": (me + k) % n_exp},
                )
                for k in range(1, n_exp)
            ]

        def finish(self):
            for c in self.copies:
                c.wait_recv()

    def w_rows(ref, lo, n):
        return ref.at[pl.ds(lo, n), :]

    whole_d, whole_h = d // 2, hs // 2
    gather_wg = Gather(
        wg_ref, lambda s: wg_buf.at[s],
        (lambda r: w_rows(r, 0, whole_d), lambda r: w_rows(r, whole_d, whole_d)), wr, wl,
    )
    gather_wu = Gather(
        wu_ref, lambda s: wu_buf.at[s],
        (lambda r: w_rows(r, 0, whole_d), lambda r: w_rows(r, whole_d, whole_d)), wr, wl,
    )
    gather_wd = Gather(
        wd_ref, lambda s: wd_buf.at[s],
        (lambda r: w_rows(r, 0, whole_h), lambda r: w_rows(r, whole_h, whole_h)), wr, wl,
    )
    experts_half = n_exp // 2
    row_halves = (
        lambda r: r.at[pl.ds(0, experts_half)],
        lambda r: r.at[pl.ds(experts_half, experts_half)],
    )
    gather_x = Gather(x_buf.at[0], lambda s: x_buf.at[s], row_halves, tr, tl)
    gather_g = Gather(g_buf.at[0], lambda s: g_buf.at[s], row_halves, tr, tl)
    deal_x = Exchange(x_send, lambda e: x_buf.at[0, e])
    deal_g = Exchange(g_send, lambda e: g_buf.at[0, e])
    scatter_out = Scatter(p_out, via_out, in_out, tr, tl)
    scatter_back = Scatter(p_back, via_back, in_back, tr, tl)
    scatter_gu = Scatter(p_gu, via_gu, in_gu, wr, wl)
    scatter_dn = Scatter(p_dn, via_dn, in_dn, wr, wl)
    home_out = Exchange(out_send, lambda e: out_home.at[e])
    home_back = Exchange(back_send, lambda e: back_home.at[e])

    pl.semaphore_wait(barrier, 4 + n_exp - 1)
    gather_wg.start()
    gather_wu.start()
    gather_wd.start()

    loads[0].wait()
    loads[1].wait()
    lane = lax.broadcasted_iota(jnp.int32, (tok, rows), 1)
    expert_of, slot_of = lane // cap, lane % cap
    token = lax.broadcasted_iota(jnp.int32, (tok, tok), 0)
    other = lax.broadcasted_iota(jnp.int32, (tok, tok), 1)

    def column_of(row):
        return jnp.sum(jnp.where(token == other, row, 0.0), axis=1, keepdims=True)

    def row_of(column):
        return jnp.sum(jnp.where(token == other, column, 0.0), axis=0, keepdims=True)

    gates = [column_of(gp_ref[k : k + 1, :]) for k in range(2)]
    choices = ids_ref[...].astype(F32)
    chosen = expert_of.astype(F32)
    named = [column_of(choices[k : k + 1, :]) == chosen for k in range(2)]
    either = (named[0] | named[1]).astype(F32).astype(BF16)
    earlier = (other < token).astype(F32).astype(BF16)
    before = jnp.dot(earlier, either, preferred_element_type=F32)
    here = before == slot_of.astype(F32)
    pick = [(named[k] & here).astype(F32).astype(BF16) for k in range(2)]
    pick_any = pick[0] + pick[1]

    def cols(n):
        return pl.ds(pl.multiple_of(n * tile, tile), tile)

    def deal_tile(n, _):
        c = cols(n)
        sent = lax.dot_general(pick_any, tok_ref[:, c], ROWS_ROWS, preferred_element_type=F32)
        x_send[:, :, c] = sent.astype(BF16).reshape(n_exp, cap, tile)
        return 0

    loads[2].wait()
    lax.fori_loop(0, n_tiles, deal_tile, 0)
    deal_x.start()
    x_buf[0, me] = x_send[me]

    def deal_grad_tile(n, _):
        c = cols(n)
        cot = cot_ref[:, c].astype(F32)
        sent = sum(
            lax.dot_general(
                pick[k], (gates[k] * cot).astype(BF16), ROWS_ROWS,
                preferred_element_type=F32,
            )
            for k in range(2)
        )
        g_send[:, :, c] = sent.astype(BF16).reshape(n_exp, cap, tile)
        return 0

    loads[3].wait()
    lax.fori_loop(0, n_tiles, deal_grad_tile, 0)
    deal_g.start()
    g_buf[0, me] = g_send[me]

    wg = [wg_buf.at[s] for s in range(RING)]
    wu = [wu_buf.at[s] for s in range(RING)]
    wd = [wd_buf.at[s] for s in range(RING)]

    gather_wg.relay()
    gather_wu.relay()
    deal_x.finish()
    gather_x.start()
    gather_wd.relay()
    deal_g.finish()
    gather_x.relay()
    gather_g.start()

    def forward(i):
        x = x_buf[i].reshape(rows, d)
        for j in range(RING):
            w = jnp.concatenate([wg[j][...], wu[j][...]], axis=1)
            pre = jnp.dot(x, w, preferred_element_type=F32)
            g, u = pre[:, :hs], pre[:, hs:]
            s = 1.0 / (1.0 + jnp.exp(-g))
            gs = g * s
            c = slice(j * hs, (j + 1) * hs)
            h = (gs * u).astype(BF16)
            h_buf[i, :, c] = h
            a_buf[i, :, c] = u * s * (1.0 + g * (1.0 - s))
            b_buf[i, :, c] = gs
            ht_buf[c, pl.ds(pl.multiple_of(i * rows, rows), rows)] = h.T

    def backward(i):
        g = g_buf[i].reshape(rows, d)
        for j in range(0, RING, 2):
            w = jnp.concatenate([wd[j][...], wd[j + 1][...]], axis=0)
            dh = lax.dot_general(g, w, COLS_COLS, preferred_element_type=F32)
            for jj in range(2):
                c = slice((j + jj) * hs, (j + jj + 1) * hs)
                part = dh[:, jj * hs : (jj + 1) * hs]
                dp = jnp.concatenate([part * a_buf[i, :, c], part * b_buf[i, :, c]], axis=1)
                dp = dp.astype(BF16)
                dp_buf[i, :, (j + jj) * 2 * hs : (j + jj + 1) * 2 * hs] = dp
                dpt_buf[j + jj, :, pl.ds(pl.multiple_of(i * rows, rows), rows)] = dp.T

    def store_rows(part, own, slot, c, value):
        if slot == 0:
            own[:, c] = value
        else:
            n = value.shape[0] // 2
            part[slot - 1, 0, :, c] = value[:n].astype(BF16)
            part[slot - 1, 1, :, c] = value[n:].astype(BF16)

    def out_part(i):
        def one(n, _):
            c = cols(n)
            w = jnp.concatenate([wd[j][:, c] for j in range(RING)], axis=0)
            store_rows(p_out, own_out, i, c, jnp.dot(h_buf[i], w, preferred_element_type=F32))
            return 0

        lax.fori_loop(0, n_tiles, one, 0)

    def back_part(i):
        def one(n, _):
            c = cols(n)
            w = jnp.concatenate(
                [r[c, :] for j in range(RING) for r in (wg[j], wu[j])], axis=1
            )
            value = lax.dot_general(dp_buf[i], w, COLS_COLS, preferred_element_type=F32)
            store_rows(p_back, own_back, i, c, value)
            return 0

        lax.fori_loop(0, n_tiles, one, 0)

    def gate_up_part(j):
        def one(n, _):
            c = cols(n)
            x = x_buf[:, :, :, c].reshape(RING * rows, tile)
            store_rows(p_gu, own_gu, j, c, jnp.dot(dpt_buf[j], x, preferred_element_type=F32))
            return 0

        lax.fori_loop(0, n_tiles, one, 0)

    def down_parts():
        def one(n, _):
            c = cols(n)
            g = g_buf[:, :, :, c].reshape(RING * rows, tile)
            value = jnp.dot(ht_buf[...], g, preferred_element_type=F32)
            for j in range(RING):
                store_rows(p_dn, own_dn, j, c, value[j * hs : (j + 1) * hs])
            return 0

        lax.fori_loop(0, n_tiles, one, 0)

    def both_sides(body):
        def step(k, _):
            body(1 + 2 * k)
            return 0

        lax.fori_loop(0, 2, step, 0)

    def total(arrived, own, sent):
        for h in range(2):
            value = (
                own[h * half : (h + 1) * half, :]
                + arrived[0, h].astype(F32)
                + arrived[1, h].astype(F32)
            )
            sent[h * experts_half : (h + 1) * experts_half] = value.astype(BF16).reshape(
                experts_half, cap, d
            )

    for load in loads[4:]:
        load.wait()
    for gather in (gather_wg, gather_wu):
        gather.sides()
        gather.finish()
    forward(0)
    gather_x.sides()
    both_sides(forward)
    gather_x.finish()
    forward(2)
    gather_g.relay()
    gather_wd.sides()
    gather_wd.finish()
    out_part(2)
    scatter_out.far()
    out_part(1)
    out_part(3)
    scatter_out.near()
    out_part(0)

    backward(0)
    gather_g.sides()
    both_sides(backward)
    scatter_out.add()
    gather_g.finish()
    backward(2)
    back_part(2)
    scatter_back.far()
    back_part(1)
    back_part(3)
    scatter_back.near()
    scatter_out.finish()
    total(in_out, own_out, out_send)
    home_out.start()
    out_home[me] = out_send[me]
    gate_up_part(2)
    scatter_back.add()
    scatter_gu.far()
    gate_up_part(1)
    gate_up_part(3)
    scatter_gu.near()
    down_parts()
    scatter_dn.far()
    scatter_dn.near()
    back_part(0)
    scatter_gu.add()
    scatter_back.finish()
    total(in_back, own_back, back_send)
    home_back.start()
    back_home[me] = back_send[me]
    gate_up_part(0)

    home_out.finish()

    def mix_tile(n, inner):
        c = cols(n)
        home = out_home[:, :, c].reshape(rows, tile)
        per = [jnp.dot(pick[k], home, preferred_element_type=F32) for k in range(2)]
        mixed_ref[:, c] = (gates[0] * per[0] + gates[1] * per[1]).astype(BF16)
        cot = cot_ref[:, c].astype(F32)
        return tuple(
            inner[k] + jnp.sum(cot * per[k], axis=1, keepdims=True) for k in range(2)
        )

    zero = jnp.zeros((tok, 1), F32)
    inner = lax.fori_loop(0, n_tiles, mix_tile, (zero, zero))
    for k in range(2):
        dgate_ref[k : k + 1, :] = row_of(inner[k])

    scatter_dn.add()
    home_back.finish()

    def home_tile(n, _):
        c = cols(n)
        home = back_home[:, :, c].reshape(rows, tile)
        dtok_ref[:, c] = jnp.dot(pick_any, home, preferred_element_type=F32).astype(BF16)
        return 0

    lax.fori_loop(0, n_tiles, home_tile, 0)

    scatter_gu.finish()
    for h, ref in enumerate((dwg_ref, dwu_ref)):
        value = (
            own_gu[h * hs : (h + 1) * hs, :]
            + in_gu[0, h].astype(F32)
            + in_gu[1, h].astype(F32)
        )
        ref[...] = value.T

    scatter_dn.finish()
    for h in range(2):
        r = slice(h * hs // 2, (h + 1) * hs // 2)
        dwd_ref[r, :] = own_dn[r, :] + in_dn[0, h].astype(F32) + in_dn[1, h].astype(F32)

    for c in started:
        c.wait_send()


def write_kernel(*refs):
    n = len(refs) // 2
    sem = refs[-1]
    copies = [pltpu.make_async_copy(refs[k], refs[n + k], sem.at[k]) for k in range(n)]
    for c in copies:
        c.start()
    for c in copies:
        c.wait()


def per_device(tokens, gate_probs, expert_ids, cotangent, gate_weight, up_weight, down_weight):
    tok, d = tokens.shape
    n_exp = lax.axis_size("expert")
    cap = 2 * tok // n_exp
    rows = 2 * tok
    hs = gate_weight.shape[2]
    hidden = RING * hs
    n_copies = 6 * 5 + 6 * 4 + 4 * (n_exp - 1)
    vmem = pltpu.VMEM
    shapes = [
        vmem((tok, d), BF16),
        vmem((tok, d), BF16),
        vmem((2, tok), F32),
        vmem((2, tok), jnp.int32),
        vmem((RING, n_exp, cap, d), BF16),
        vmem((RING, n_exp, cap, d), BF16),
        vmem((RING, d, hs), BF16),
        vmem((RING, d, hs), BF16),
        vmem((RING, hs, d), BF16),
        vmem((n_exp, cap, d), BF16),
        vmem((n_exp, cap, d), BF16),
        vmem((RING, rows, hidden), F32),
        vmem((RING, rows, hidden), F32),
        vmem((RING, rows, hidden), BF16),
        vmem((hidden, RING * rows), BF16),
        vmem((RING, rows, 2 * hidden), BF16),
        vmem((RING, 2 * hs, RING * rows), BF16),
    ]
    heights = (rows, rows, 2 * hs, hs)
    shapes += [vmem((3, 2, n // 2, d), BF16) for n in heights]
    shapes += [vmem((2, n // 2, d), BF16) for n in heights]
    shapes += [vmem((2, 2, n // 2, d), BF16) for n in heights]
    shapes += [vmem((n, d), F32) for n in heights]
    shapes += [vmem((n_exp, cap, d), BF16) for _ in range(4)]
    shapes += [pltpu.SemaphoreType.DMA((n,)) for n in (n_copies, n_copies, 7)]
    here, away = pl.BlockSpec(memory_space=pltpu.VMEM), pl.BlockSpec(memory_space=pl.ANY)
    results = [
        ((tok, d), BF16), ((tok, d), BF16), ((2, tok), F32),
        ((d, hs), F32), ((d, hs), F32), ((hs, d), F32),
    ]
    inside = pl.pallas_call(
        functools.partial(layer_kernel, n_exp),
        out_shape=[pltpu.VMEM(*r) for r in results],
        in_specs=[away] * 7,
        out_specs=[here] * len(results),
        scratch_shapes=shapes,
        compiler_params=pltpu.CompilerParams(
            collective_id=0, has_side_effects=True, vmem_limit_bytes=58 * 1024 * 1024
        ),
    )(
        tokens, gate_probs.T, expert_ids.T, cotangent,
        gate_weight[0], up_weight[0], down_weight[0],
    )
    mixed, d_tokens, d_gates, d_gate_w, d_up_w, d_down = pl.pallas_call(
        write_kernel,
        out_shape=[jax.ShapeDtypeStruct(*r) for r in results],
        in_specs=[here] * len(results),
        out_specs=[away] * len(results),
        scratch_shapes=[pltpu.SemaphoreType.DMA((len(results),))],
        compiler_params=pltpu.CompilerParams(vmem_limit_bytes=1024 * 1024),
    )(*inside)
    return mixed, d_tokens, d_gates.T, d_gate_w[None], d_up_w[None], d_down[None]


def solution(mesh):
    rows = P(("expert", "fsdp"), None)
    hidden = P("expert", None, "fsdp")
    hidden_rows = P("expert", "fsdp", None)
    return jax.shard_map(
        per_device,
        mesh=mesh,
        in_specs=(rows, rows, rows, rows, hidden, hidden, hidden_rows),
        out_specs=(rows, rows, rows, hidden, hidden, hidden_rows),
        check_vma=False,
    )
```

```python
import functools

import jax
import jax.numpy as jnp
from jax import lax
from jax.experimental import pallas as pl
from jax.experimental.pallas import tpu as pltpu
from jax.sharding import PartitionSpec as P

MESH = pl.DeviceIdType.MESH
F32, BF16 = jnp.float32, jnp.bfloat16
RING = 4
ROWS_ROWS = (((0,), (0,)), ((), ()))
COLS_COLS = (((1,), (1,)), ((), ()))


def layer_kernel(
    n_exp,
    tok_hbm, gp_hbm, ids_hbm, cot_hbm, wg_ref, wu_ref, wd_ref,
    mixed_ref, dtok_ref, dgate_ref, dwg_ref, dwu_ref, dwd_ref,
    tok_ref, cot_ref, gp_ref, ids_ref, x_buf, g_buf, wg_buf, wu_buf, wd_buf, x_send, g_send,
    a_buf, b_buf, h_buf, ht_buf, dp_buf, dpt_buf,
    p_out, p_back, p_gu, p_dn,
    via_out, via_back, via_gu, via_dn,
    in_out, in_back, in_gu, in_dn,
    own_out, own_back, own_gu, own_dn,
    out_send, back_send, out_home, back_home,
    send_sem, recv_sem, load_sem,
):
    tok, d = tok_ref.shape
    cap = 2 * tok // n_exp
    rows = n_exp * cap
    hs = wg_ref.shape[1]
    half = rows // 2
    tile = min(256, d)
    n_tiles = d // tile

    me = lax.axis_index("expert")
    f = lax.axis_index("fsdp")
    core = me % 2
    z, y = f // RING, f % RING
    along_z_up, along_z_down = ((z + 1) % RING) * RING + y, ((z + 3) % RING) * RING + y
    along_y_up, along_y_down = z * RING + (y + 1) % RING, z * RING + (y + 3) % RING
    t_right = along_z_up * (1 - core) + along_y_up * core
    t_left = along_z_down * (1 - core) + along_y_down * core
    w_right = along_y_up * (1 - core) + along_z_up * core
    w_left = along_y_down * (1 - core) + along_z_down * core
    tr, tl = {"fsdp": t_right}, {"fsdp": t_left}
    wr, wl = {"fsdp": w_right}, {"fsdp": w_left}

    barrier = pltpu.get_barrier_semaphore()
    for dev in (tr, tl, wr, wl):
        pl.semaphore_signal(barrier, inc=1, device_id=dev, device_id_type=MESH)
    for k in range(1, n_exp):
        pl.semaphore_signal(
            barrier, inc=1, device_id={"expert": (me + k) % n_exp}, device_id_type=MESH
        )

    loads = [
        pltpu.make_async_copy(src, dst, load_sem.at[n])
        for n, (src, dst) in enumerate(
            [
                (ids_hbm, ids_ref), (gp_hbm, gp_ref), (tok_hbm, tok_ref), (cot_hbm, cot_ref),
                (wg_ref, wg_buf.at[0]), (wu_ref, wu_buf.at[0]), (wd_ref, wd_buf.at[0]),
            ]
        )
    ]
    for load in loads:
        load.start()

    flows = []
    used = [0, 0]

    def take(which, n):
        first = used[which]
        used[which] += n
        return first

    class Flow:
        def __init__(self, n_recv, bytes_out):
            self.out, self.into = take(0, 1), take(1, n_recv)
            self.bytes_out = bytes_out
            flows.append(self)

        def descriptor(self, src, dst, n, dev):
            return pltpu.make_async_remote_copy(
                src_ref=src, dst_ref=dst, send_sem=send_sem.at[self.out],
                recv_sem=recv_sem.at[self.into + n], device_id=dev, device_id_type=MESH,
            )

        def send(self, src, dst, n, dev):
            self.descriptor(src, dst, n, dev).start()

        def arrive(self, ref, n):
            self.descriptor(ref, ref, n, tr).wait_recv()

        def sent(self):
            self.descriptor(self.bytes_out, self.bytes_out, 0, tr).wait_send()

    class Gather(Flow):
        def __init__(self, own, buf, halves, right, left):
            super().__init__(4, buf.at[pl.ds(1, RING - 1)])
            self.own, self.slot, self.halves = own, lambda k: buf.at[k], halves
            self.right, self.left = right, left

        def start(self):
            lo, hi = self.halves
            self.send(lo(self.own), lo(self.slot(1)), 0, self.right)
            self.send(hi(self.own), hi(self.slot(3)), 1, self.left)
            self.send(hi(self.own), hi(self.slot(1)), 2, self.right)
            self.send(lo(self.own), lo(self.slot(3)), 2, self.left)

        def relay(self):
            lo, hi = self.halves
            self.arrive(lo(self.slot(1)), 0)
            self.send(lo(self.slot(1)), lo(self.slot(2)), 3, self.right)
            self.arrive(hi(self.slot(3)), 1)
            self.send(hi(self.slot(3)), hi(self.slot(2)), 3, self.left)

        def sides(self):
            self.arrive(self.slot(1), 2)

        def finish(self):
            self.arrive(self.slot(2), 3)

    class Scatter(Flow):
        def __init__(self, part, via, arrived, right, left):
            super().__init__(3, part)
            self.part, self.via, self.arrived = part, via, arrived
            self.right, self.left = right, left

        def far(self):
            self.send(self.part.at[1, 0], self.via.at[0], 0, self.right)
            self.send(self.part.at[1, 1], self.via.at[1], 1, self.left)

        def near(self):
            self.send(self.part.at[2, 1], self.arrived.at[0, 1], 2, self.right)
            self.send(self.part.at[0, 0], self.arrived.at[1, 0], 2, self.left)

        def add(self):
            def plus(slot, h):
                total = self.part[slot, h].astype(F32) + self.via[h].astype(F32)
                self.part[slot, h] = total.astype(BF16)

            self.arrive(self.via.at[0], 0)
            plus(2, 0)
            self.send(self.part.at[2, 0], self.arrived.at[0, 0], 2, self.right)
            self.arrive(self.via.at[1], 1)
            plus(0, 1)
            self.send(self.part.at[0, 1], self.arrived.at[1, 1], 2, self.left)

        def finish(self):
            self.arrive(self.arrived, 2)

    class Exchange(Flow):
        def __init__(self, src, dst):
            super().__init__(1, src.at[pl.ds(0, n_exp - 1)])
            self.src, self.dst = src, dst

        def start(self):
            for k in range(1, n_exp):
                peer = (me + k) % n_exp
                self.send(self.src.at[peer], self.dst.at[me], 0, {"expert": peer})

        def finish(self):
            self.arrive(self.dst.at[pl.ds(0, n_exp - 1)], 0)

    def w_rows(ref, lo, n):
        return ref.at[pl.ds(lo, n), :]

    whole_d, whole_h = d // 2, hs // 2
    gather_wg = Gather(
        wg_ref, wg_buf,
        (lambda r: w_rows(r, 0, whole_d), lambda r: w_rows(r, whole_d, whole_d)), wr, wl,
    )
    gather_wu = Gather(
        wu_ref, wu_buf,
        (lambda r: w_rows(r, 0, whole_d), lambda r: w_rows(r, whole_d, whole_d)), wr, wl,
    )
    gather_wd = Gather(
        wd_ref, wd_buf,
        (lambda r: w_rows(r, 0, whole_h), lambda r: w_rows(r, whole_h, whole_h)), wr, wl,
    )
    experts_half = n_exp // 2
    row_halves = (
        lambda r: r.at[pl.ds(0, experts_half)],
        lambda r: r.at[pl.ds(experts_half, experts_half)],
    )
    gather_x = Gather(x_buf.at[0], x_buf, row_halves, tr, tl)
    gather_g = Gather(g_buf.at[0], g_buf, row_halves, tr, tl)
    deal_x = Exchange(x_send, x_buf.at[0])
    deal_g = Exchange(g_send, g_buf.at[0])
    scatter_out = Scatter(p_out, via_out, in_out, tr, tl)
    scatter_back = Scatter(p_back, via_back, in_back, tr, tl)
    scatter_gu = Scatter(p_gu, via_gu, in_gu, wr, wl)
    scatter_dn = Scatter(p_dn, via_dn, in_dn, wr, wl)
    home_out = Exchange(out_send, out_home)
    home_back = Exchange(back_send, back_home)

    pl.semaphore_wait(barrier, 4 + n_exp - 1)
    gather_wg.start()
    gather_wu.start()
    gather_wd.start()

    loads[0].wait()
    loads[1].wait()
    lane = lax.broadcasted_iota(jnp.int32, (tok, rows), 1)
    expert_of, slot_of = lane // cap, lane % cap
    token = lax.broadcasted_iota(jnp.int32, (tok, tok), 0)
    other = lax.broadcasted_iota(jnp.int32, (tok, tok), 1)

    def column_of(row):
        return jnp.sum(jnp.where(token == other, row, 0.0), axis=1, keepdims=True)

    def row_of(column):
        return jnp.sum(jnp.where(token == other, column, 0.0), axis=0, keepdims=True)

    gates = [column_of(gp_ref[k : k + 1, :]) for k in range(2)]
    choices = ids_ref[...].astype(F32)
    chosen = expert_of.astype(F32)
    named = [column_of(choices[k : k + 1, :]) == chosen for k in range(2)]
    either = (named[0] | named[1]).astype(F32).astype(BF16)
    earlier = (other < token).astype(F32).astype(BF16)
    before = jnp.dot(earlier, either, preferred_element_type=F32)
    here = before == slot_of.astype(F32)
    pick = [(named[k] & here).astype(F32).astype(BF16) for k in range(2)]
    pick_any = pick[0] + pick[1]

    def cols(n):
        return pl.ds(pl.multiple_of(n * tile, tile), tile)

    def deal_tile(n, _):
        c = cols(n)
        sent = lax.dot_general(pick_any, tok_ref[:, c], ROWS_ROWS, preferred_element_type=F32)
        x_send[:, :, c] = sent.astype(BF16).reshape(n_exp, cap, tile)
        return 0

    loads[2].wait()
    lax.fori_loop(0, n_tiles, deal_tile, 0)
    deal_x.start()
    x_buf[0, me] = x_send[me]

    def deal_grad_tile(n, _):
        c = cols(n)
        cot = cot_ref[:, c].astype(F32)
        sent = sum(
            lax.dot_general(
                pick[k], (gates[k] * cot).astype(BF16), ROWS_ROWS,
                preferred_element_type=F32,
            )
            for k in range(2)
        )
        g_send[:, :, c] = sent.astype(BF16).reshape(n_exp, cap, tile)
        return 0

    loads[3].wait()
    lax.fori_loop(0, n_tiles, deal_grad_tile, 0)
    deal_g.start()
    g_buf[0, me] = g_send[me]

    wg = [wg_buf.at[s] for s in range(RING)]
    wu = [wu_buf.at[s] for s in range(RING)]
    wd = [wd_buf.at[s] for s in range(RING)]

    gather_wg.relay()
    gather_wu.relay()
    deal_x.finish()
    gather_x.start()
    gather_wd.relay()
    deal_g.finish()
    gather_x.relay()
    gather_g.start()

    def forward(i):
        x = x_buf[i].reshape(rows, d)
        for j in range(RING):
            w = jnp.concatenate([wg[j][...], wu[j][...]], axis=1)
            pre = jnp.dot(x, w, preferred_element_type=F32)
            g, u = pre[:, :hs], pre[:, hs:]
            s = 1.0 / (1.0 + jnp.exp(-g))
            gs = g * s
            c = slice(j * hs, (j + 1) * hs)
            h = (gs * u).astype(BF16)
            h_buf[i, :, c] = h
            a_buf[i, :, c] = u * s * (1.0 + g * (1.0 - s))
            b_buf[i, :, c] = gs
            ht_buf[c, pl.ds(pl.multiple_of(i * rows, rows), rows)] = h.T

    def backward(i):
        g = g_buf[i].reshape(rows, d)
        for j in range(0, RING, 2):
            w = jnp.concatenate([wd[j][...], wd[j + 1][...]], axis=0)
            dh = lax.dot_general(g, w, COLS_COLS, preferred_element_type=F32)
            for jj in range(2):
                c = slice((j + jj) * hs, (j + jj + 1) * hs)
                part = dh[:, jj * hs : (jj + 1) * hs]
                dp = jnp.concatenate([part * a_buf[i, :, c], part * b_buf[i, :, c]], axis=1)
                dp = dp.astype(BF16)
                dp_buf[i, :, (j + jj) * 2 * hs : (j + jj + 1) * 2 * hs] = dp
                dpt_buf[j + jj, :, pl.ds(pl.multiple_of(i * rows, rows), rows)] = dp.T

    def store_rows(part, own, slot, c, value):
        if slot == 0:
            own[:, c] = value
        else:
            n = value.shape[0] // 2
            part[slot - 1, 0, :, c] = value[:n].astype(BF16)
            part[slot - 1, 1, :, c] = value[n:].astype(BF16)

    def out_part(i):
        def one(n, _):
            c = cols(n)
            w = jnp.concatenate([wd[j][:, c] for j in range(RING)], axis=0)
            store_rows(p_out, own_out, i, c, jnp.dot(h_buf[i], w, preferred_element_type=F32))
            return 0

        lax.fori_loop(0, n_tiles, one, 0)

    def back_part(i):
        def one(n, _):
            c = cols(n)
            w = jnp.concatenate(
                [r[c, :] for j in range(RING) for r in (wg[j], wu[j])], axis=1
            )
            value = lax.dot_general(dp_buf[i], w, COLS_COLS, preferred_element_type=F32)
            store_rows(p_back, own_back, i, c, value)
            return 0

        lax.fori_loop(0, n_tiles, one, 0)

    def gate_up_part(j):
        def one(n, _):
            c = cols(n)
            x = x_buf[:, :, :, c].reshape(RING * rows, tile)
            store_rows(p_gu, own_gu, j, c, jnp.dot(dpt_buf[j], x, preferred_element_type=F32))
            return 0

        lax.fori_loop(0, n_tiles, one, 0)

    def down_parts():
        def one(n, _):
            c = cols(n)
            g = g_buf[:, :, :, c].reshape(RING * rows, tile)
            value = jnp.dot(ht_buf[...], g, preferred_element_type=F32)
            for j in range(RING):
                store_rows(p_dn, own_dn, j, c, value[j * hs : (j + 1) * hs])
            return 0

        lax.fori_loop(0, n_tiles, one, 0)

    def both_sides(body):
        def step(k, _):
            body(1 + 2 * k)
            return 0

        lax.fori_loop(0, 2, step, 0)

    def total(arrived, own, sent):
        for h in range(2):
            value = (
                own[h * half : (h + 1) * half, :]
                + arrived[0, h].astype(F32)
                + arrived[1, h].astype(F32)
            )
            sent[h * experts_half : (h + 1) * experts_half] = value.astype(BF16).reshape(
                experts_half, cap, d
            )

    for load in loads[4:]:
        load.wait()
    for gather in (gather_wg, gather_wu):
        gather.sides()
        gather.finish()
    forward(0)
    gather_x.sides()
    both_sides(forward)
    gather_x.finish()
    forward(2)
    gather_g.relay()
    gather_wd.sides()
    gather_wd.finish()
    out_part(2)
    scatter_out.far()
    out_part(1)
    out_part(3)
    scatter_out.near()
    out_part(0)

    backward(0)
    gather_g.sides()
    both_sides(backward)
    scatter_out.add()
    gather_g.finish()
    backward(2)
    back_part(2)
    scatter_back.far()
    back_part(1)
    back_part(3)
    scatter_back.near()
    scatter_out.finish()
    total(in_out, own_out, out_send)
    home_out.start()
    out_home[me] = out_send[me]
    gate_up_part(2)
    scatter_back.add()
    scatter_gu.far()
    gate_up_part(1)
    gate_up_part(3)
    scatter_gu.near()
    down_parts()
    scatter_dn.far()
    scatter_dn.near()
    back_part(0)
    scatter_gu.add()
    scatter_back.finish()
    total(in_back, own_back, back_send)
    home_back.start()
    back_home[me] = back_send[me]
    gate_up_part(0)

    home_out.finish()

    def mix_tile(n, inner):
        c = cols(n)
        home = out_home[:, :, c].reshape(rows, tile)
        per = [jnp.dot(pick[k], home, preferred_element_type=F32) for k in range(2)]
        mixed_ref[:, c] = (gates[0] * per[0] + gates[1] * per[1]).astype(BF16)
        cot = cot_ref[:, c].astype(F32)
        return tuple(
            inner[k] + jnp.sum(cot * per[k], axis=1, keepdims=True) for k in range(2)
        )

    zero = jnp.zeros((tok, 1), F32)
    inner = lax.fori_loop(0, n_tiles, mix_tile, (zero, zero))
    for k in range(2):
        dgate_ref[k : k + 1, :] = row_of(inner[k])

    scatter_dn.add()
    home_back.finish()

    def home_tile(n, _):
        c = cols(n)
        home = back_home[:, :, c].reshape(rows, tile)
        dtok_ref[:, c] = jnp.dot(pick_any, home, preferred_element_type=F32).astype(BF16)
        return 0

    lax.fori_loop(0, n_tiles, home_tile, 0)

    scatter_gu.finish()
    for h, ref in enumerate((dwg_ref, dwu_ref)):
        value = (
            own_gu[h * hs : (h + 1) * hs, :]
            + in_gu[0, h].astype(F32)
            + in_gu[1, h].astype(F32)
        )
        ref[...] = value.T

    scatter_dn.finish()
    for h in range(2):
        r = slice(h * hs // 2, (h + 1) * hs // 2)
        dwd_ref[r, :] = own_dn[r, :] + in_dn[0, h].astype(F32) + in_dn[1, h].astype(F32)

    for flow in flows:
        flow.sent()


def write_kernel(*refs):
    n = len(refs) // 2
    sem = refs[-1]
    copies = [pltpu.make_async_copy(refs[k], refs[n + k], sem.at[k]) for k in range(n)]
    for c in copies:
        c.start()
    for c in copies:
        c.wait()


def per_device(tokens, gate_probs, expert_ids, cotangent, gate_weight, up_weight, down_weight):
    tok, d = tokens.shape
    n_exp = lax.axis_size("expert")
    cap = 2 * tok // n_exp
    rows = 2 * tok
    hs = gate_weight.shape[2]
    hidden = RING * hs
    n_out, n_in = 5 + 4 + 4, 4 * 5 + 3 * 4 + 4
    vmem = pltpu.VMEM
    shapes = [
        vmem((tok, d), BF16),
        vmem((tok, d), BF16),
        vmem((2, tok), F32),
        vmem((2, tok), jnp.int32),
        vmem((RING, n_exp, cap, d), BF16),
        vmem((RING, n_exp, cap, d), BF16),
        vmem((RING, d, hs), BF16),
        vmem((RING, d, hs), BF16),
        vmem((RING, hs, d), BF16),
        vmem((n_exp, cap, d), BF16),
        vmem((n_exp, cap, d), BF16),
        vmem((RING, rows, hidden), F32),
        vmem((RING, rows, hidden), F32),
        vmem((RING, rows, hidden), BF16),
        vmem((hidden, RING * rows), BF16),
        vmem((RING, rows, 2 * hidden), BF16),
        vmem((RING, 2 * hs, RING * rows), BF16),
    ]
    heights = (rows, rows, 2 * hs, hs)
    shapes += [vmem((3, 2, n // 2, d), BF16) for n in heights]
    shapes += [vmem((2, n // 2, d), BF16) for n in heights]
    shapes += [vmem((2, 2, n // 2, d), BF16) for n in heights]
    shapes += [vmem((n, d), F32) for n in heights]
    shapes += [vmem((n_exp, cap, d), BF16) for _ in range(4)]
    shapes += [pltpu.SemaphoreType.DMA((n,)) for n in (n_out, n_in, 7)]
    here, away = pl.BlockSpec(memory_space=pltpu.VMEM), pl.BlockSpec(memory_space=pl.ANY)
    results = [
        ((tok, d), BF16), ((tok, d), BF16), ((2, tok), F32),
        ((d, hs), F32), ((d, hs), F32), ((hs, d), F32),
    ]
    inside = pl.pallas_call(
        functools.partial(layer_kernel, n_exp),
        out_shape=[pltpu.VMEM(*r) for r in results],
        in_specs=[away] * 7,
        out_specs=[here] * len(results),
        scratch_shapes=shapes,
        compiler_params=pltpu.CompilerParams(
            collective_id=0, has_side_effects=True, vmem_limit_bytes=58 * 1024 * 1024
        ),
    )(
        tokens, gate_probs.T, expert_ids.T, cotangent,
        gate_weight[0], up_weight[0], down_weight[0],
    )
    mixed, d_tokens, d_gates, d_gate_w, d_up_w, d_down = pl.pallas_call(
        write_kernel,
        out_shape=[jax.ShapeDtypeStruct(*r) for r in results],
        in_specs=[here] * len(results),
        out_specs=[away] * len(results),
        scratch_shapes=[pltpu.SemaphoreType.DMA((len(results),))],
        compiler_params=pltpu.CompilerParams(vmem_limit_bytes=1024 * 1024),
    )(*inside)
    return mixed, d_tokens, d_gates.T, d_gate_w[None], d_up_w[None], d_down[None]


def solution(mesh):
    rows = P(("expert", "fsdp"), None)
    hidden = P("expert", None, "fsdp")
    hidden_rows = P("expert", "fsdp", None)
    return jax.shard_map(
        per_device,
        mesh=mesh,
        in_specs=(rows, rows, rows, rows, hidden, hidden, hidden_rows),
        out_specs=(rows, rows, rows, hidden, hidden, hidden_rows),
        check_vma=False,
    )
```

```python
import functools

import jax
import jax.numpy as jnp
from jax import lax
from jax.experimental import pallas as pl
from jax.experimental.pallas import tpu as pltpu
from jax.sharding import PartitionSpec as P

MESH = pl.DeviceIdType.MESH
F32, BF16 = jnp.float32, jnp.bfloat16
RING = 4
ROWS_ROWS = (((0,), (0,)), ((), ()))
COLS_COLS = (((1,), (1,)), ((), ()))


def layer_kernel(
    n_exp,
    tok_hbm, gp_hbm, ids_hbm, cot_hbm, wg_ref, wu_ref, wd_ref,
    mixed_ref, dtok_ref, dgate_ref, dwg_ref, dwu_ref, dwd_ref,
    tok_ref, cot_ref, gp_ref, ids_ref, x_buf, g_buf, wg_buf, wu_buf, wd_buf, x_send, g_send,
    a_buf, b_buf, h_buf, ht_buf, dp_buf, dpt_buf,
    p_out, p_back, p_gu, p_dn,
    via_out, via_back, via_gu, via_dn,
    in_out, in_back, in_gu, in_dn,
    own_out, own_back, own_gu, own_dn,
    out_send, back_send, out_home, back_home,
    send_sem, recv_sem, load_sem,
):
    tok, d = tok_ref.shape
    cap = 2 * tok // n_exp
    rows = n_exp * cap
    hs = wg_ref.shape[1]
    half = rows // 2
    tile = min(256, d)
    n_tiles = d // tile

    me = lax.axis_index("expert")
    f = lax.axis_index("fsdp")
    core = me % 2
    z, y = f // RING, f % RING
    along_z_up, along_z_down = ((z + 1) % RING) * RING + y, ((z + 3) % RING) * RING + y
    along_y_up, along_y_down = z * RING + (y + 1) % RING, z * RING + (y + 3) % RING
    t_right = along_z_up * (1 - core) + along_y_up * core
    t_left = along_z_down * (1 - core) + along_y_down * core
    w_right = along_y_up * (1 - core) + along_z_up * core
    w_left = along_y_down * (1 - core) + along_z_down * core
    tr, tl = {"fsdp": t_right}, {"fsdp": t_left}
    wr, wl = {"fsdp": w_right}, {"fsdp": w_left}

    barrier = pltpu.get_barrier_semaphore()
    for dev in (tr, tl, wr, wl):
        pl.semaphore_signal(barrier, inc=1, device_id=dev, device_id_type=MESH)
    for k in range(1, n_exp):
        pl.semaphore_signal(
            barrier, inc=1, device_id={"expert": (me + k) % n_exp}, device_id_type=MESH
        )

    loads = [
        pltpu.make_async_copy(src, dst, load_sem.at[n])
        for n, (src, dst) in enumerate(
            [
                (wg_ref, wg_buf.at[0]), (ids_hbm, ids_ref), (gp_hbm, gp_ref),
                (tok_hbm, tok_ref), (wu_ref, wu_buf.at[0]), (wd_ref, wd_buf.at[0]),
                (cot_hbm, cot_ref),
            ]
        )
    ]
    for load in loads:
        load.start()

    flows = []
    used = [0, 0]

    def take(which, n):
        first = used[which]
        used[which] += n
        return first

    class Flow:
        def __init__(self, n_recv, bytes_out):
            self.out, self.into = take(0, 1), take(1, n_recv)
            self.bytes_out = bytes_out
            flows.append(self)

        def descriptor(self, src, dst, n, dev):
            return pltpu.make_async_remote_copy(
                src_ref=src, dst_ref=dst, send_sem=send_sem.at[self.out],
                recv_sem=recv_sem.at[self.into + n], device_id=dev, device_id_type=MESH,
            )

        def send(self, src, dst, n, dev):
            self.descriptor(src, dst, n, dev).start()

        def arrive(self, ref, n):
            self.descriptor(ref, ref, n, tr).wait_recv()

        def sent(self):
            self.descriptor(self.bytes_out, self.bytes_out, 0, tr).wait_send()

    class Gather(Flow):
        def __init__(self, own, buf, halves, right, left):
            super().__init__(4, buf.at[pl.ds(1, RING - 1)])
            self.own, self.slot, self.halves = own, lambda k: buf.at[k], halves
            self.right, self.left = right, left

        def start(self):
            lo, hi = self.halves
            self.send(lo(self.own), lo(self.slot(1)), 0, self.right)
            self.send(hi(self.own), hi(self.slot(3)), 1, self.left)
            self.send(hi(self.own), hi(self.slot(1)), 2, self.right)
            self.send(lo(self.own), lo(self.slot(3)), 2, self.left)

        def relay(self):
            lo, hi = self.halves
            self.arrive(lo(self.slot(1)), 0)
            self.send(lo(self.slot(1)), lo(self.slot(2)), 3, self.right)
            self.arrive(hi(self.slot(3)), 1)
            self.send(hi(self.slot(3)), hi(self.slot(2)), 3, self.left)

        def sides(self):
            self.arrive(self.slot(1), 2)

        def finish(self):
            self.arrive(self.slot(2), 3)

    class Scatter(Flow):
        def __init__(self, part, via, arrived, right, left):
            super().__init__(3, part)
            self.part, self.via, self.arrived = part, via, arrived
            self.right, self.left = right, left

        def far(self):
            self.send(self.part.at[1, 0], self.via.at[0], 0, self.right)
            self.send(self.part.at[1, 1], self.via.at[1], 1, self.left)

        def near(self):
            self.send(self.part.at[2, 1], self.arrived.at[0, 1], 2, self.right)
            self.send(self.part.at[0, 0], self.arrived.at[1, 0], 2, self.left)

        def add(self):
            def plus(slot, h):
                total = self.part[slot, h].astype(F32) + self.via[h].astype(F32)
                self.part[slot, h] = total.astype(BF16)

            self.arrive(self.via.at[0], 0)
            plus(2, 0)
            self.send(self.part.at[2, 0], self.arrived.at[0, 0], 2, self.right)
            self.arrive(self.via.at[1], 1)
            plus(0, 1)
            self.send(self.part.at[0, 1], self.arrived.at[1, 1], 2, self.left)

        def finish(self):
            self.arrive(self.arrived, 2)

    class Exchange(Flow):
        def __init__(self, src, dst):
            super().__init__(1, src.at[pl.ds(0, n_exp - 1)])
            self.src, self.dst = src, dst

        def start(self):
            for k in range(1, n_exp):
                peer = (me + k) % n_exp
                self.send(self.src.at[peer], self.dst.at[me], 0, {"expert": peer})

        def finish(self):
            self.arrive(self.dst.at[pl.ds(0, n_exp - 1)], 0)

    def w_rows(ref, lo, n):
        return ref.at[pl.ds(lo, n), :]

    whole_d, whole_h = d // 2, hs // 2
    gather_wg = Gather(
        wg_buf.at[0], wg_buf,
        (lambda r: w_rows(r, 0, whole_d), lambda r: w_rows(r, whole_d, whole_d)), wr, wl,
    )
    gather_wu = Gather(
        wu_buf.at[0], wu_buf,
        (lambda r: w_rows(r, 0, whole_d), lambda r: w_rows(r, whole_d, whole_d)), wr, wl,
    )
    gather_wd = Gather(
        wd_buf.at[0], wd_buf,
        (lambda r: w_rows(r, 0, whole_h), lambda r: w_rows(r, whole_h, whole_h)), wr, wl,
    )
    experts_half = n_exp // 2
    row_halves = (
        lambda r: r.at[pl.ds(0, experts_half)],
        lambda r: r.at[pl.ds(experts_half, experts_half)],
    )
    gather_x = Gather(x_buf.at[0], x_buf, row_halves, tr, tl)
    gather_g = Gather(g_buf.at[0], g_buf, row_halves, tr, tl)
    deal_x = Exchange(x_send, x_buf.at[0])
    deal_g = Exchange(g_send, g_buf.at[0])
    scatter_out = Scatter(p_out, via_out, in_out, tr, tl)
    scatter_back = Scatter(p_back, via_back, in_back, tr, tl)
    scatter_gu = Scatter(p_gu, via_gu, in_gu, wr, wl)
    scatter_dn = Scatter(p_dn, via_dn, in_dn, wr, wl)
    home_out = Exchange(out_send, out_home)
    home_back = Exchange(back_send, back_home)

    pl.semaphore_wait(barrier, 4 + n_exp - 1)
    for load, gather in ((0, gather_wg), (4, gather_wu), (5, gather_wd)):
        loads[load].wait()
        gather.start()

    loads[1].wait()
    loads[2].wait()
    lane = lax.broadcasted_iota(jnp.int32, (tok, rows), 1)
    expert_of, slot_of = lane // cap, lane % cap
    token = lax.broadcasted_iota(jnp.int32, (tok, tok), 0)
    other = lax.broadcasted_iota(jnp.int32, (tok, tok), 1)

    def column_of(row):
        return jnp.sum(jnp.where(token == other, row, 0.0), axis=1, keepdims=True)

    def row_of(column):
        return jnp.sum(jnp.where(token == other, column, 0.0), axis=0, keepdims=True)

    gates = [column_of(gp_ref[k : k + 1, :]) for k in range(2)]
    choices = ids_ref[...].astype(F32)
    chosen = expert_of.astype(F32)
    named = [column_of(choices[k : k + 1, :]) == chosen for k in range(2)]
    either = (named[0] | named[1]).astype(F32).astype(BF16)
    earlier = (other < token).astype(F32).astype(BF16)
    before = jnp.dot(earlier, either, preferred_element_type=F32)
    here = before == slot_of.astype(F32)
    pick = [(named[k] & here).astype(F32).astype(BF16) for k in range(2)]
    pick_any = pick[0] + pick[1]

    def cols(n):
        return pl.ds(pl.multiple_of(n * tile, tile), tile)

    def deal_tile(n, _):
        c = cols(n)
        sent = lax.dot_general(pick_any, tok_ref[:, c], ROWS_ROWS, preferred_element_type=F32)
        x_send[:, :, c] = sent.astype(BF16).reshape(n_exp, cap, tile)
        return 0

    loads[3].wait()
    lax.fori_loop(0, n_tiles, deal_tile, 0)
    deal_x.start()
    x_buf[0, me] = x_send[me]

    def deal_grad_tile(n, _):
        c = cols(n)
        cot = cot_ref[:, c].astype(F32)
        sent = sum(
            lax.dot_general(
                pick[k], (gates[k] * cot).astype(BF16), ROWS_ROWS,
                preferred_element_type=F32,
            )
            for k in range(2)
        )
        g_send[:, :, c] = sent.astype(BF16).reshape(n_exp, cap, tile)
        return 0

    loads[6].wait()
    lax.fori_loop(0, n_tiles, deal_grad_tile, 0)
    deal_g.start()
    g_buf[0, me] = g_send[me]

    wg = [wg_buf.at[s] for s in range(RING)]
    wu = [wu_buf.at[s] for s in range(RING)]
    wd = [wd_buf.at[s] for s in range(RING)]

    gather_wg.relay()
    gather_wu.relay()
    deal_x.finish()
    gather_x.start()
    gather_wd.relay()
    deal_g.finish()
    gather_x.relay()
    gather_g.start()

    def forward(i):
        x = x_buf[i].reshape(rows, d)
        for j in range(RING):
            w = jnp.concatenate([wg[j][...], wu[j][...]], axis=1)
            pre = jnp.dot(x, w, preferred_element_type=F32)
            g, u = pre[:, :hs], pre[:, hs:]
            s = 1.0 / (1.0 + jnp.exp(-g))
            gs = g * s
            c = slice(j * hs, (j + 1) * hs)
            h = (gs * u).astype(BF16)
            h_buf[i, :, c] = h
            a_buf[i, :, c] = u * s * (1.0 + g * (1.0 - s))
            b_buf[i, :, c] = gs
            ht_buf[c, pl.ds(pl.multiple_of(i * rows, rows), rows)] = h.T

    def backward(i):
        g = g_buf[i].reshape(rows, d)
        for j in range(0, RING, 2):
            w = jnp.concatenate([wd[j][...], wd[j + 1][...]], axis=0)
            dh = lax.dot_general(g, w, COLS_COLS, preferred_element_type=F32)
            for jj in range(2):
                c = slice((j + jj) * hs, (j + jj + 1) * hs)
                part = dh[:, jj * hs : (jj + 1) * hs]
                dp = jnp.concatenate([part * a_buf[i, :, c], part * b_buf[i, :, c]], axis=1)
                dp = dp.astype(BF16)
                dp_buf[i, :, (j + jj) * 2 * hs : (j + jj + 1) * 2 * hs] = dp
                dpt_buf[j + jj, :, pl.ds(pl.multiple_of(i * rows, rows), rows)] = dp.T

    def store_rows(part, own, slot, c, value):
        if slot == 0:
            own[:, c] = value
        else:
            n = value.shape[0] // 2
            part[slot - 1, 0, :, c] = value[:n].astype(BF16)
            part[slot - 1, 1, :, c] = value[n:].astype(BF16)

    def out_part(i):
        def one(n, _):
            c = cols(n)
            w = jnp.concatenate([wd[j][:, c] for j in range(RING)], axis=0)
            store_rows(p_out, own_out, i, c, jnp.dot(h_buf[i], w, preferred_element_type=F32))
            return 0

        lax.fori_loop(0, n_tiles, one, 0)

    def back_part(i):
        def one(n, _):
            c = cols(n)
            w = jnp.concatenate(
                [r[c, :] for j in range(RING) for r in (wg[j], wu[j])], axis=1
            )
            value = lax.dot_general(dp_buf[i], w, COLS_COLS, preferred_element_type=F32)
            store_rows(p_back, own_back, i, c, value)
            return 0

        lax.fori_loop(0, n_tiles, one, 0)

    def gate_up_part(j):
        def one(n, _):
            c = cols(n)
            x = x_buf[:, :, :, c].reshape(RING * rows, tile)
            store_rows(p_gu, own_gu, j, c, jnp.dot(dpt_buf[j], x, preferred_element_type=F32))
            return 0

        lax.fori_loop(0, n_tiles, one, 0)

    def down_parts():
        def one(n, _):
            c = cols(n)
            g = g_buf[:, :, :, c].reshape(RING * rows, tile)
            value = jnp.dot(ht_buf[...], g, preferred_element_type=F32)
            for j in range(RING):
                store_rows(p_dn, own_dn, j, c, value[j * hs : (j + 1) * hs])
            return 0

        lax.fori_loop(0, n_tiles, one, 0)

    def both_sides(body):
        def step(k, _):
            body(1 + 2 * k)
            return 0

        lax.fori_loop(0, 2, step, 0)

    def total(arrived, own, sent):
        for h in range(2):
            value = (
                own[h * half : (h + 1) * half, :]
                + arrived[0, h].astype(F32)
                + arrived[1, h].astype(F32)
            )
            sent[h * experts_half : (h + 1) * experts_half] = value.astype(BF16).reshape(
                experts_half, cap, d
            )

    for gather in (gather_wg, gather_wu):
        gather.sides()
        gather.finish()
    forward(0)
    gather_x.sides()
    both_sides(forward)
    gather_x.finish()
    forward(2)
    gather_g.relay()
    gather_wd.sides()
    gather_wd.finish()
    out_part(2)
    scatter_out.far()
    out_part(1)
    out_part(3)
    scatter_out.near()
    out_part(0)

    backward(0)
    gather_g.sides()
    both_sides(backward)
    scatter_out.add()
    gather_g.finish()
    backward(2)
    back_part(2)
    scatter_back.far()
    back_part(1)
    back_part(3)
    scatter_back.near()
    scatter_out.finish()
    total(in_out, own_out, out_send)
    home_out.start()
    out_home[me] = out_send[me]
    gate_up_part(2)
    scatter_back.add()
    scatter_gu.far()
    gate_up_part(1)
    gate_up_part(3)
    scatter_gu.near()
    down_parts()
    scatter_dn.far()
    scatter_dn.near()
    back_part(0)
    scatter_gu.add()
    scatter_back.finish()
    total(in_back, own_back, back_send)
    home_back.start()
    back_home[me] = back_send[me]
    gate_up_part(0)

    home_out.finish()

    def mix_tile(n, inner):
        c = cols(n)
        home = out_home[:, :, c].reshape(rows, tile)
        per = [jnp.dot(pick[k], home, preferred_element_type=F32) for k in range(2)]
        mixed_ref[:, c] = (gates[0] * per[0] + gates[1] * per[1]).astype(BF16)
        cot = cot_ref[:, c].astype(F32)
        return tuple(
            inner[k] + jnp.sum(cot * per[k], axis=1, keepdims=True) for k in range(2)
        )

    zero = jnp.zeros((tok, 1), F32)
    inner = lax.fori_loop(0, n_tiles, mix_tile, (zero, zero))
    for k in range(2):
        dgate_ref[k : k + 1, :] = row_of(inner[k])

    scatter_dn.add()
    home_back.finish()

    def home_tile(n, _):
        c = cols(n)
        home = back_home[:, :, c].reshape(rows, tile)
        dtok_ref[:, c] = jnp.dot(pick_any, home, preferred_element_type=F32).astype(BF16)
        return 0

    lax.fori_loop(0, n_tiles, home_tile, 0)

    scatter_gu.finish()
    for h, ref in enumerate((dwg_ref, dwu_ref)):
        value = (
            own_gu[h * hs : (h + 1) * hs, :]
            + in_gu[0, h].astype(F32)
            + in_gu[1, h].astype(F32)
        )
        ref[...] = value.T

    scatter_dn.finish()
    for h in range(2):
        r = slice(h * hs // 2, (h + 1) * hs // 2)
        dwd_ref[r, :] = own_dn[r, :] + in_dn[0, h].astype(F32) + in_dn[1, h].astype(F32)

    for flow in flows:
        flow.sent()


def write_kernel(*refs):
    n = len(refs) // 2
    sem = refs[-1]
    copies = [pltpu.make_async_copy(refs[k], refs[n + k], sem.at[k]) for k in range(n)]
    for c in copies:
        c.start()
    for c in copies:
        c.wait()


def per_device(tokens, gate_probs, expert_ids, cotangent, gate_weight, up_weight, down_weight):
    tok, d = tokens.shape
    n_exp = lax.axis_size("expert")
    cap = 2 * tok // n_exp
    rows = 2 * tok
    hs = gate_weight.shape[2]
    hidden = RING * hs
    n_out, n_in = 5 + 4 + 4, 4 * 5 + 3 * 4 + 4
    vmem = pltpu.VMEM
    shapes = [
        vmem((tok, d), BF16),
        vmem((tok, d), BF16),
        vmem((2, tok), F32),
        vmem((2, tok), jnp.int32),
        vmem((RING, n_exp, cap, d), BF16),
        vmem((RING, n_exp, cap, d), BF16),
        vmem((RING, d, hs), BF16),
        vmem((RING, d, hs), BF16),
        vmem((RING, hs, d), BF16),
        vmem((n_exp, cap, d), BF16),
        vmem((n_exp, cap, d), BF16),
        vmem((RING, rows, hidden), F32),
        vmem((RING, rows, hidden), F32),
        vmem((RING, rows, hidden), BF16),
        vmem((hidden, RING * rows), BF16),
        vmem((RING, rows, 2 * hidden), BF16),
        vmem((RING, 2 * hs, RING * rows), BF16),
    ]
    heights = (rows, rows, 2 * hs, hs)
    shapes += [vmem((3, 2, n // 2, d), BF16) for n in heights]
    shapes += [vmem((2, n // 2, d), BF16) for n in heights]
    shapes += [vmem((2, 2, n // 2, d), BF16) for n in heights]
    shapes += [vmem((n, d), F32) for n in heights]
    shapes += [vmem((n_exp, cap, d), BF16) for _ in range(4)]
    shapes += [pltpu.SemaphoreType.DMA((n,)) for n in (n_out, n_in, 7)]
    here, away = pl.BlockSpec(memory_space=pltpu.VMEM), pl.BlockSpec(memory_space=pl.ANY)
    results = [
        ((tok, d), BF16), ((tok, d), BF16), ((2, tok), F32),
        ((d, hs), F32), ((d, hs), F32), ((hs, d), F32),
    ]
    inside = pl.pallas_call(
        functools.partial(layer_kernel, n_exp),
        out_shape=[pltpu.VMEM(*r) for r in results],
        in_specs=[away] * 7,
        out_specs=[here] * len(results),
        scratch_shapes=shapes,
        compiler_params=pltpu.CompilerParams(
            collective_id=0, has_side_effects=True, vmem_limit_bytes=58 * 1024 * 1024
        ),
    )(
        tokens, gate_probs.T, expert_ids.T, cotangent,
        gate_weight[0], up_weight[0], down_weight[0],
    )
    mixed, d_tokens, d_gates, d_gate_w, d_up_w, d_down = pl.pallas_call(
        write_kernel,
        out_shape=[jax.ShapeDtypeStruct(*r) for r in results],
        in_specs=[here] * len(results),
        out_specs=[away] * len(results),
        scratch_shapes=[pltpu.SemaphoreType.DMA((len(results),))],
        compiler_params=pltpu.CompilerParams(vmem_limit_bytes=1024 * 1024),
    )(*inside)
    return mixed, d_tokens, d_gates.T, d_gate_w[None], d_up_w[None], d_down[None]


def solution(mesh):
    rows = P(("expert", "fsdp"), None)
    hidden = P("expert", None, "fsdp")
    hidden_rows = P("expert", "fsdp", None)
    return jax.shard_map(
        per_device,
        mesh=mesh,
        in_specs=(rows, rows, rows, rows, hidden, hidden, hidden_rows),
        out_specs=(rows, rows, rows, hidden, hidden, hidden_rows),
        check_vma=False,
    )
```

```python
import functools

import jax
import jax.numpy as jnp
from jax import lax
from jax.experimental import pallas as pl
from jax.experimental.pallas import tpu as pltpu
from jax.sharding import PartitionSpec as P

MESH = pl.DeviceIdType.MESH
F32, BF16 = jnp.float32, jnp.bfloat16
RING = 4
ROWS_ROWS = (((0,), (0,)), ((), ()))
COLS_COLS = (((1,), (1,)), ((), ()))


def layer_kernel(
    n_exp,
    tok_hbm, gp_hbm, ids_hbm, cot_hbm, wg_ref, wu_ref, wd_ref,
    mixed_ref, dtok_ref, dgate_ref, dwg_ref, dwu_ref, dwd_ref,
    tok_ref, cot_ref, gp_ref, ids_ref, x_buf, g_buf, wg_buf, wu_buf, wd_buf, x_send, g_send,
    a_buf, b_buf, h_buf, ht_buf, dp_buf, dpt_buf,
    p_out, p_back, p_gu, p_dn,
    via_out, via_back, via_gu, via_dn,
    in_out, in_back, in_gu, in_dn,
    own_out, own_back, own_gu, own_dn,
    out_send, back_send, out_home, back_home,
    send_sem, recv_sem, load_sem,
):
    tok, d = tok_ref.shape
    cap = 2 * tok // n_exp
    rows = n_exp * cap
    hs = wg_ref.shape[1]
    half = rows // 2
    tile = min(256, d)
    n_tiles = d // tile

    me = lax.axis_index("expert")
    f = lax.axis_index("fsdp")
    core = me % 2
    z, y = f // RING, f % RING
    along_z_up, along_z_down = ((z + 1) % RING) * RING + y, ((z + 3) % RING) * RING + y
    along_y_up, along_y_down = z * RING + (y + 1) % RING, z * RING + (y + 3) % RING
    t_right = along_z_up * (1 - core) + along_y_up * core
    t_left = along_z_down * (1 - core) + along_y_down * core
    w_right = along_y_up * (1 - core) + along_z_up * core
    w_left = along_y_down * (1 - core) + along_z_down * core
    tr, tl = {"fsdp": t_right}, {"fsdp": t_left}
    wr, wl = {"fsdp": w_right}, {"fsdp": w_left}

    barrier = pltpu.get_barrier_semaphore()
    for dev in (tr, tl, wr, wl):
        pl.semaphore_signal(barrier, inc=1, device_id=dev, device_id_type=MESH)
    for k in range(1, n_exp):
        pl.semaphore_signal(
            barrier, inc=1, device_id={"expert": (me + k) % n_exp}, device_id_type=MESH
        )

    loads = [
        pltpu.make_async_copy(src, dst, load_sem.at[n])
        for n, (src, dst) in enumerate(
            [
                (wg_ref, wg_buf.at[0]), (ids_hbm, ids_ref), (gp_hbm, gp_ref),
                (tok_hbm, tok_ref), (wu_ref, wu_buf.at[0]), (wd_ref, wd_buf.at[0]),
                (cot_hbm, cot_ref),
            ]
        )
    ]
    for load in loads:
        load.start()

    flows = []
    used = [0, 0]

    def take(which, n):
        first = used[which]
        used[which] += n
        return first

    class Flow:
        def __init__(self, n_recv, bytes_out, into=None):
            self.out = take(0, 1)
            self.into = take(1, n_recv) if into is None else into
            self.bytes_out = bytes_out
            flows.append(self)

        def descriptor(self, src, dst, n, dev):
            return pltpu.make_async_remote_copy(
                src_ref=src, dst_ref=dst, send_sem=send_sem.at[self.out],
                recv_sem=recv_sem.at[self.into + n], device_id=dev, device_id_type=MESH,
            )

        def send(self, src, dst, n, dev):
            self.descriptor(src, dst, n, dev).start()

        def arrive(self, ref, n):
            self.descriptor(ref, ref, n, tr).wait_recv()

        def sent(self):
            self.descriptor(self.bytes_out, self.bytes_out, 0, tr).wait_send()

    class Gather(Flow):
        def __init__(self, own, buf, halves, right, left, into=None):
            super().__init__(4, buf.at[pl.ds(1, RING - 1)], into)
            self.own, self.slot, self.halves = own, lambda k: buf.at[k], halves
            self.right, self.left = right, left

        def start(self):
            self.start_first()
            self.start_second()

        def start_first(self):
            lo, hi = self.halves
            self.send(lo(self.own), lo(self.slot(1)), 0, self.right)
            self.send(hi(self.own), hi(self.slot(3)), 1, self.left)

        def start_second(self):
            lo, hi = self.halves
            self.send(hi(self.own), hi(self.slot(1)), 2, self.right)
            self.send(lo(self.own), lo(self.slot(3)), 2, self.left)

        def relay_right(self):
            lo, _ = self.halves
            self.send(lo(self.slot(1)), lo(self.slot(2)), 3, self.right)

        def relay_left(self):
            _, hi = self.halves
            self.send(hi(self.slot(3)), hi(self.slot(2)), 3, self.left)

        def relay(self):
            lo, hi = self.halves
            self.arrive(lo(self.slot(1)), 0)
            self.relay_right()
            self.arrive(hi(self.slot(3)), 1)
            self.relay_left()

        def sides(self):
            self.arrive(self.slot(1), 2)

        def finish(self):
            self.arrive(self.slot(2), 3)

    class Scatter(Flow):
        def __init__(self, part, via, arrived, right, left):
            super().__init__(3, part)
            self.part, self.via, self.arrived = part, via, arrived
            self.right, self.left = right, left

        def far(self):
            self.send(self.part.at[1, 0], self.via.at[0], 0, self.right)
            self.send(self.part.at[1, 1], self.via.at[1], 1, self.left)

        def near(self):
            self.send(self.part.at[2, 1], self.arrived.at[0, 1], 2, self.right)
            self.send(self.part.at[0, 0], self.arrived.at[1, 0], 2, self.left)

        def add(self):
            def plus(slot, h):
                total = self.part[slot, h].astype(F32) + self.via[h].astype(F32)
                self.part[slot, h] = total.astype(BF16)

            self.arrive(self.via.at[0], 0)
            plus(2, 0)
            self.send(self.part.at[2, 0], self.arrived.at[0, 0], 2, self.right)
            self.arrive(self.via.at[1], 1)
            plus(0, 1)
            self.send(self.part.at[0, 1], self.arrived.at[1, 1], 2, self.left)

        def finish(self):
            self.arrive(self.arrived, 2)

    class Exchange(Flow):
        def __init__(self, src, dst):
            super().__init__(1, src.at[pl.ds(0, n_exp - 1)])
            self.src, self.dst = src, dst

        def start(self):
            for k in range(1, n_exp):
                peer = (me + k) % n_exp
                self.send(self.src.at[peer], self.dst.at[me], 0, {"expert": peer})

        def finish(self):
            self.arrive(self.dst.at[pl.ds(0, n_exp - 1)], 0)

    def w_rows(ref, lo, n):
        return ref.at[pl.ds(lo, n), :]

    whole_d, whole_h = d // 2, hs // 2
    gather_wg = Gather(
        wg_buf.at[0], wg_buf,
        (lambda r: w_rows(r, 0, whole_d), lambda r: w_rows(r, whole_d, whole_d)), wr, wl,
    )
    gather_wu = Gather(
        wu_buf.at[0], wu_buf,
        (lambda r: w_rows(r, 0, whole_d), lambda r: w_rows(r, whole_d, whole_d)), wr, wl,
        gather_wg.into,
    )
    gather_wd = Gather(
        wd_buf.at[0], wd_buf,
        (lambda r: w_rows(r, 0, whole_h), lambda r: w_rows(r, whole_h, whole_h)), wr, wl,
        gather_wg.into,
    )
    weights = (gather_wg, gather_wu, gather_wd)
    experts_half = n_exp // 2
    row_halves = (
        lambda r: r.at[pl.ds(0, experts_half)],
        lambda r: r.at[pl.ds(experts_half, experts_half)],
    )
    gather_x = Gather(x_buf.at[0], x_buf, row_halves, tr, tl)
    gather_g = Gather(g_buf.at[0], g_buf, row_halves, tr, tl)
    deal_x = Exchange(x_send, x_buf.at[0])
    deal_g = Exchange(g_send, g_buf.at[0])
    scatter_out = Scatter(p_out, via_out, in_out, tr, tl)
    scatter_back = Scatter(p_back, via_back, in_back, tr, tl)
    scatter_gu = Scatter(p_gu, via_gu, in_gu, wr, wl)
    scatter_dn = Scatter(p_dn, via_dn, in_dn, wr, wl)
    home_out = Exchange(out_send, out_home)
    home_back = Exchange(back_send, back_home)

    pl.semaphore_wait(barrier, 4 + n_exp - 1)
    for load, gather in zip((0, 4, 5), weights):
        loads[load].wait()
        gather.start_first()
    for gather in weights:
        gather.start_second()

    loads[1].wait()
    loads[2].wait()
    lane = lax.broadcasted_iota(jnp.int32, (tok, rows), 1)
    expert_of, slot_of = lane // cap, lane % cap
    token = lax.broadcasted_iota(jnp.int32, (tok, tok), 0)
    other = lax.broadcasted_iota(jnp.int32, (tok, tok), 1)

    def column_of(row):
        return jnp.sum(jnp.where(token == other, row, 0.0), axis=1, keepdims=True)

    def row_of(column):
        return jnp.sum(jnp.where(token == other, column, 0.0), axis=0, keepdims=True)

    gates = [column_of(gp_ref[k : k + 1, :]) for k in range(2)]
    choices = ids_ref[...].astype(F32)
    chosen = expert_of.astype(F32)
    named = [column_of(choices[k : k + 1, :]) == chosen for k in range(2)]
    either = (named[0] | named[1]).astype(F32).astype(BF16)
    earlier = (other < token).astype(F32).astype(BF16)
    before = jnp.dot(earlier, either, preferred_element_type=F32)
    here = before == slot_of.astype(F32)
    pick = [(named[k] & here).astype(F32).astype(BF16) for k in range(2)]
    pick_any = pick[0] + pick[1]

    def cols(n):
        return pl.ds(pl.multiple_of(n * tile, tile), tile)

    def deal_tile(n, _):
        c = cols(n)
        sent = lax.dot_general(pick_any, tok_ref[:, c], ROWS_ROWS, preferred_element_type=F32)
        x_send[:, :, c] = sent.astype(BF16).reshape(n_exp, cap, tile)
        return 0

    loads[3].wait()
    lax.fori_loop(0, n_tiles, deal_tile, 0)
    deal_x.start()
    x_buf[0, me] = x_send[me]

    def deal_grad_tile(n, _):
        c = cols(n)
        cot = cot_ref[:, c].astype(F32)
        sent = sum(
            lax.dot_general(
                pick[k], (gates[k] * cot).astype(BF16), ROWS_ROWS,
                preferred_element_type=F32,
            )
            for k in range(2)
        )
        g_send[:, :, c] = sent.astype(BF16).reshape(n_exp, cap, tile)
        return 0

    loads[6].wait()
    lax.fori_loop(0, n_tiles, deal_grad_tile, 0)
    deal_g.start()
    g_buf[0, me] = g_send[me]

    wg = [wg_buf.at[s] for s in range(RING)]
    wu = [wu_buf.at[s] for s in range(RING)]
    wd = [wd_buf.at[s] for s in range(RING)]

    halves_in = wg_buf.at[pl.ds(1, 3), pl.ds(0, whole_d)]
    gather_wg.arrive(halves_in, 0)
    for gather in weights:
        gather.relay_right()
    gather_wg.arrive(halves_in, 1)
    for gather in weights:
        gather.relay_left()
    deal_x.finish()
    gather_x.start()
    deal_g.finish()
    gather_x.relay()
    gather_g.start()

    def forward(i):
        x = x_buf[i].reshape(rows, d)
        for j in range(RING):
            w = jnp.concatenate([wg[j][...], wu[j][...]], axis=1)
            pre = jnp.dot(x, w, preferred_element_type=F32)
            g, u = pre[:, :hs], pre[:, hs:]
            s = 1.0 / (1.0 + jnp.exp(-g))
            gs = g * s
            c = slice(j * hs, (j + 1) * hs)
            h = (gs * u).astype(BF16)
            h_buf[i, :, c] = h
            a_buf[i, :, c] = u * s * (1.0 + g * (1.0 - s))
            b_buf[i, :, c] = gs
            ht_buf[c, pl.ds(pl.multiple_of(i * rows, rows), rows)] = h.T

    def backward(i):
        g = g_buf[i].reshape(rows, d)
        for j in range(0, RING, 2):
            w = jnp.concatenate([wd[j][...], wd[j + 1][...]], axis=0)
            dh = lax.dot_general(g, w, COLS_COLS, preferred_element_type=F32)
            for jj in range(2):
                c = slice((j + jj) * hs, (j + jj + 1) * hs)
                part = dh[:, jj * hs : (jj + 1) * hs]
                dp = jnp.concatenate([part * a_buf[i, :, c], part * b_buf[i, :, c]], axis=1)
                dp = dp.astype(BF16)
                dp_buf[i, :, (j + jj) * 2 * hs : (j + jj + 1) * 2 * hs] = dp
                dpt_buf[j + jj, :, pl.ds(pl.multiple_of(i * rows, rows), rows)] = dp.T

    def store_rows(part, own, slot, c, value):
        if slot == 0:
            own[:, c] = value
        else:
            n = value.shape[0] // 2
            part[slot - 1, 0, :, c] = value[:n].astype(BF16)
            part[slot - 1, 1, :, c] = value[n:].astype(BF16)

    def out_part(i):
        def one(n, _):
            c = cols(n)
            w = jnp.concatenate([wd[j][:, c] for j in range(RING)], axis=0)
            store_rows(p_out, own_out, i, c, jnp.dot(h_buf[i], w, preferred_element_type=F32))
            return 0

        lax.fori_loop(0, n_tiles, one, 0)

    def back_part(i):
        def one(n, _):
            c = cols(n)
            w = jnp.concatenate(
                [r[c, :] for j in range(RING) for r in (wg[j], wu[j])], axis=1
            )
            value = lax.dot_general(dp_buf[i], w, COLS_COLS, preferred_element_type=F32)
            store_rows(p_back, own_back, i, c, value)
            return 0

        lax.fori_loop(0, n_tiles, one, 0)

    def gate_up_part(j):
        def one(n, _):
            c = cols(n)
            x = x_buf[:, :, :, c].reshape(RING * rows, tile)
            store_rows(p_gu, own_gu, j, c, jnp.dot(dpt_buf[j], x, preferred_element_type=F32))
            return 0

        lax.fori_loop(0, n_tiles, one, 0)

    def down_parts():
        def one(n, _):
            c = cols(n)
            g = g_buf[:, :, :, c].reshape(RING * rows, tile)
            value = jnp.dot(ht_buf[...], g, preferred_element_type=F32)
            for j in range(RING):
                store_rows(p_dn, own_dn, j, c, value[j * hs : (j + 1) * hs])
            return 0

        lax.fori_loop(0, n_tiles, one, 0)

    def both_sides(body):
        def step(k, _):
            body(1 + 2 * k)
            return 0

        lax.fori_loop(0, 2, step, 0)

    def total(arrived, own, sent):
        for h in range(2):
            value = (
                own[h * half : (h + 1) * half, :]
                + arrived[0, h].astype(F32)
                + arrived[1, h].astype(F32)
            )
            sent[h * experts_half : (h + 1) * experts_half] = value.astype(BF16).reshape(
                experts_half, cap, d
            )

    blocks_in = wg_buf.at[pl.ds(1, 3)]
    for n in (2, 3):
        gather_wg.arrive(blocks_in, n)
    forward(0)
    gather_x.sides()
    both_sides(forward)
    gather_x.finish()
    forward(2)
    gather_g.relay()
    out_part(2)
    scatter_out.far()
    out_part(1)
    out_part(3)
    scatter_out.near()
    out_part(0)

    backward(0)
    gather_g.sides()
    both_sides(backward)
    scatter_out.add()
    gather_g.finish()
    backward(2)
    back_part(2)
    scatter_back.far()
    back_part(1)
    back_part(3)
    scatter_back.near()
    scatter_out.finish()
    total(in_out, own_out, out_send)
    home_out.start()
    out_home[me] = out_send[me]
    gate_up_part(2)
    scatter_back.add()
    scatter_gu.far()
    gate_up_part(1)
    gate_up_part(3)
    scatter_gu.near()
    down_parts()
    scatter_dn.far()
    scatter_dn.near()
    back_part(0)
    scatter_gu.add()
    scatter_back.finish()
    total(in_back, own_back, back_send)
    home_back.start()
    back_home[me] = back_send[me]
    gate_up_part(0)

    home_out.finish()

    def mix_tile(n, inner):
        c = cols(n)
        home = out_home[:, :, c].reshape(rows, tile)
        per = [jnp.dot(pick[k], home, preferred_element_type=F32) for k in range(2)]
        mixed_ref[:, c] = (gates[0] * per[0] + gates[1] * per[1]).astype(BF16)
        cot = cot_ref[:, c].astype(F32)
        return tuple(
            inner[k] + jnp.sum(cot * per[k], axis=1, keepdims=True) for k in range(2)
        )

    zero = jnp.zeros((tok, 1), F32)
    inner = lax.fori_loop(0, n_tiles, mix_tile, (zero, zero))
    for k in range(2):
        dgate_ref[k : k + 1, :] = row_of(inner[k])

    scatter_dn.add()
    home_back.finish()

    def home_tile(n, _):
        c = cols(n)
        home = back_home[:, :, c].reshape(rows, tile)
        dtok_ref[:, c] = jnp.dot(pick_any, home, preferred_element_type=F32).astype(BF16)
        return 0

    lax.fori_loop(0, n_tiles, home_tile, 0)

    scatter_gu.finish()
    for h, ref in enumerate((dwg_ref, dwu_ref)):
        value = (
            own_gu[h * hs : (h + 1) * hs, :]
            + in_gu[0, h].astype(F32)
            + in_gu[1, h].astype(F32)
        )
        ref[...] = value.T

    scatter_dn.finish()
    for h in range(2):
        r = slice(h * hs // 2, (h + 1) * hs // 2)
        dwd_ref[r, :] = own_dn[r, :] + in_dn[0, h].astype(F32) + in_dn[1, h].astype(F32)

    for flow in flows:
        flow.sent()


def write_kernel(*refs):
    n = len(refs) // 2
    sem = refs[-1]
    copies = [pltpu.make_async_copy(refs[k], refs[n + k], sem.at[k]) for k in range(n)]
    for c in copies:
        c.start()
    for c in copies:
        c.wait()


def per_device(tokens, gate_probs, expert_ids, cotangent, gate_weight, up_weight, down_weight):
    tok, d = tokens.shape
    n_exp = lax.axis_size("expert")
    cap = 2 * tok // n_exp
    rows = 2 * tok
    hs = gate_weight.shape[2]
    hidden = RING * hs
    n_out, n_in = 5 + 4 + 4, 4 * 3 + 3 * 4 + 4
    vmem = pltpu.VMEM
    shapes = [
        vmem((tok, d), BF16),
        vmem((tok, d), BF16),
        vmem((2, tok), F32),
        vmem((2, tok), jnp.int32),
        vmem((RING, n_exp, cap, d), BF16),
        vmem((RING, n_exp, cap, d), BF16),
        vmem((RING, d, hs), BF16),
        vmem((RING, d, hs), BF16),
        vmem((RING, hs, d), BF16),
        vmem((n_exp, cap, d), BF16),
        vmem((n_exp, cap, d), BF16),
        vmem((RING, rows, hidden), F32),
        vmem((RING, rows, hidden), F32),
        vmem((RING, rows, hidden), BF16),
        vmem((hidden, RING * rows), BF16),
        vmem((RING, rows, 2 * hidden), BF16),
        vmem((RING, 2 * hs, RING * rows), BF16),
    ]
    heights = (rows, rows, 2 * hs, hs)
    shapes += [vmem((3, 2, n // 2, d), BF16) for n in heights]
    shapes += [vmem((2, n // 2, d), BF16) for n in heights]
    shapes += [vmem((2, 2, n // 2, d), BF16) for n in heights]
    shapes += [vmem((n, d), F32) for n in heights]
    shapes += [vmem((n_exp, cap, d), BF16) for _ in range(4)]
    shapes += [pltpu.SemaphoreType.DMA((n,)) for n in (n_out, n_in, 7)]
    here, away = pl.BlockSpec(memory_space=pltpu.VMEM), pl.BlockSpec(memory_space=pl.ANY)
    results = [
        ((tok, d), BF16), ((tok, d), BF16), ((2, tok), F32),
        ((d, hs), F32), ((d, hs), F32), ((hs, d), F32),
    ]
    inside = pl.pallas_call(
        functools.partial(layer_kernel, n_exp),
        out_shape=[pltpu.VMEM(*r) for r in results],
        in_specs=[away] * 7,
        out_specs=[here] * len(results),
        scratch_shapes=shapes,
        compiler_params=pltpu.CompilerParams(
            collective_id=0, has_side_effects=True, vmem_limit_bytes=58 * 1024 * 1024
        ),
    )(
        tokens, gate_probs.T, expert_ids.T, cotangent,
        gate_weight[0], up_weight[0], down_weight[0],
    )
    mixed, d_tokens, d_gates, d_gate_w, d_up_w, d_down = pl.pallas_call(
        write_kernel,
        out_shape=[jax.ShapeDtypeStruct(*r) for r in results],
        in_specs=[here] * len(results),
        out_specs=[away] * len(results),
        scratch_shapes=[pltpu.SemaphoreType.DMA((len(results),))],
        compiler_params=pltpu.CompilerParams(vmem_limit_bytes=1024 * 1024),
    )(*inside)
    return mixed, d_tokens, d_gates.T, d_gate_w[None], d_up_w[None], d_down[None]


def solution(mesh):
    rows = P(("expert", "fsdp"), None)
    hidden = P("expert", None, "fsdp")
    hidden_rows = P("expert", "fsdp", None)
    return jax.shard_map(
        per_device,
        mesh=mesh,
        in_specs=(rows, rows, rows, rows, hidden, hidden, hidden_rows),
        out_specs=(rows, rows, rows, hidden, hidden, hidden_rows),
        check_vma=False,
    )
```

```python
import functools

import jax
import jax.numpy as jnp
from jax import lax
from jax.experimental import pallas as pl
from jax.experimental.pallas import tpu as pltpu
from jax.sharding import PartitionSpec as P

MESH = pl.DeviceIdType.MESH
F32, BF16 = jnp.float32, jnp.bfloat16
RING = 4
ROWS_ROWS = (((0,), (0,)), ((), ()))
COLS_COLS = (((1,), (1,)), ((), ()))


def layer_kernel(
    n_exp,
    tok_hbm, gp_hbm, ids_hbm, cot_hbm, wg_ref, wu_ref, wd_ref,
    mixed_ref, dtok_ref, dgate_ref, dwg_ref, dwu_ref, dwd_ref,
    tok_ref, cot_ref, gp_ref, ids_ref, x_buf, g_buf, wg_buf, wu_buf, wd_buf, x_send, g_send,
    a_buf, b_buf, h_buf, ht_buf, dp_buf, dpt_buf,
    p_out, p_back, p_gu, p_dn,
    via_out, via_back, via_gu, via_dn,
    in_out, in_back, in_gu, in_dn,
    own_out, own_back, own_gu, own_dn,
    out_send, back_send, out_home, back_home,
    send_sem, recv_sem, load_sem,
):
    tok, d = tok_ref.shape
    cap = 2 * tok // n_exp
    rows = n_exp * cap
    hs = wg_ref.shape[1]
    half = rows // 2
    tile = min(256, d)
    n_tiles = d // tile

    me = lax.axis_index("expert")
    f = lax.axis_index("fsdp")
    core = me % 2
    z, y = f // RING, f % RING
    along_z_up, along_z_down = ((z + 1) % RING) * RING + y, ((z + 3) % RING) * RING + y
    along_y_up, along_y_down = z * RING + (y + 1) % RING, z * RING + (y + 3) % RING
    t_right = along_z_up * (1 - core) + along_y_up * core
    t_left = along_z_down * (1 - core) + along_y_down * core
    w_right = along_y_up * (1 - core) + along_z_up * core
    w_left = along_y_down * (1 - core) + along_z_down * core
    tr, tl = {"fsdp": t_right}, {"fsdp": t_left}
    wr, wl = {"fsdp": w_right}, {"fsdp": w_left}

    barrier = pltpu.get_barrier_semaphore()
    for dev in (tr, tl, wr, wl):
        pl.semaphore_signal(barrier, inc=1, device_id=dev, device_id_type=MESH)
    for k in range(1, n_exp):
        pl.semaphore_signal(
            barrier, inc=1, device_id={"expert": (me + k) % n_exp}, device_id_type=MESH
        )

    loads = [
        pltpu.make_async_copy(src, dst, load_sem.at[n])
        for n, (src, dst) in enumerate(
            [
                (wg_ref, wg_buf.at[0]), (ids_hbm, ids_ref), (gp_hbm, gp_ref),
                (tok_hbm, tok_ref), (wu_ref, wu_buf.at[0]), (wd_ref, wd_buf.at[0]),
                (cot_hbm, cot_ref),
            ]
        )
    ]
    for load in loads:
        load.start()

    flows = []
    used = [0, 0]

    def take(which, n):
        first = used[which]
        used[which] += n
        return first

    class Flow:
        def __init__(self, n_recv, bytes_out):
            self.out, self.into = take(0, 1), take(1, n_recv)
            self.bytes_out = bytes_out
            flows.append(self)

        def descriptor(self, src, dst, n, dev):
            return pltpu.make_async_remote_copy(
                src_ref=src, dst_ref=dst, send_sem=send_sem.at[self.out],
                recv_sem=recv_sem.at[self.into + n], device_id=dev, device_id_type=MESH,
            )

        def send(self, src, dst, n, dev):
            self.descriptor(src, dst, n, dev).start()

        def arrive(self, ref, n):
            self.descriptor(ref, ref, n, tr).wait_recv()

        def sent(self):
            self.descriptor(self.bytes_out, self.bytes_out, 0, tr).wait_send()

    class Gather(Flow):
        def __init__(self, own, buf, halves, right, left):
            super().__init__(4, buf.at[pl.ds(1, RING - 1)])
            self.own, self.slot, self.halves = own, lambda k: buf.at[k], halves
            self.right, self.left = right, left

        def start(self):
            lo, hi = self.halves
            self.send(lo(self.own), lo(self.slot(1)), 0, self.right)
            self.send(hi(self.own), hi(self.slot(3)), 1, self.left)
            self.send(hi(self.own), hi(self.slot(1)), 2, self.right)
            self.send(lo(self.own), lo(self.slot(3)), 2, self.left)

        def relay(self):
            lo, hi = self.halves
            self.arrive(lo(self.slot(1)), 0)
            self.send(lo(self.slot(1)), lo(self.slot(2)), 3, self.right)
            self.arrive(hi(self.slot(3)), 1)
            self.send(hi(self.slot(3)), hi(self.slot(2)), 3, self.left)

        def sides(self):
            self.arrive(self.slot(1), 2)

        def finish(self):
            self.arrive(self.slot(2), 3)

    class Scatter(Flow):
        def __init__(self, part, via, arrived, right, left):
            super().__init__(3, part)
            self.part, self.via, self.arrived = part, via, arrived
            self.right, self.left = right, left

        def far(self):
            self.send(self.part.at[1, 0], self.via.at[0], 0, self.right)
            self.send(self.part.at[1, 1], self.via.at[1], 1, self.left)

        def near(self):
            self.send(self.part.at[2, 1], self.arrived.at[0, 1], 2, self.right)
            self.send(self.part.at[0, 0], self.arrived.at[1, 0], 2, self.left)

        def add(self):
            def plus(slot, h):
                total = self.part[slot, h].astype(F32) + self.via[h].astype(F32)
                self.part[slot, h] = total.astype(BF16)

            self.arrive(self.via.at[0], 0)
            plus(2, 0)
            self.send(self.part.at[2, 0], self.arrived.at[0, 0], 2, self.right)
            self.arrive(self.via.at[1], 1)
            plus(0, 1)
            self.send(self.part.at[0, 1], self.arrived.at[1, 1], 2, self.left)

        def finish(self):
            self.arrive(self.arrived, 2)

    class Exchange(Flow):
        def __init__(self, src, dst):
            super().__init__(1, src.at[pl.ds(0, n_exp - 1)])
            self.src, self.dst = src, dst

        def start(self):
            for k in range(1, n_exp):
                peer = (me + k) % n_exp
                self.send(self.src.at[peer], self.dst.at[me], 0, {"expert": peer})

        def finish(self):
            self.arrive(self.dst.at[pl.ds(0, n_exp - 1)], 0)

    def w_rows(ref, lo, n):
        return ref.at[pl.ds(lo, n), :]

    whole_d, whole_h = d // 2, hs // 2
    gather_wg = Gather(
        wg_buf.at[0], wg_buf,
        (lambda r: w_rows(r, 0, whole_d), lambda r: w_rows(r, whole_d, whole_d)), wr, wl,
    )
    gather_wu = Gather(
        wu_buf.at[0], wu_buf,
        (lambda r: w_rows(r, 0, whole_d), lambda r: w_rows(r, whole_d, whole_d)), wr, wl,
    )
    gather_wd = Gather(
        wd_buf.at[0], wd_buf,
        (lambda r: w_rows(r, 0, whole_h), lambda r: w_rows(r, whole_h, whole_h)), wr, wl,
    )
    experts_half = n_exp // 2
    row_halves = (
        lambda r: r.at[pl.ds(0, experts_half)],
        lambda r: r.at[pl.ds(experts_half, experts_half)],
    )
    gather_x = Gather(x_buf.at[0], x_buf, row_halves, tr, tl)
    gather_g = Gather(g_buf.at[0], g_buf, row_halves, tr, tl)
    deal_x = Exchange(x_send, x_buf.at[0])
    deal_g = Exchange(g_send, g_buf.at[0])
    scatter_out = Scatter(p_out, via_out, in_out, tr, tl)
    scatter_back = Scatter(p_back, via_back, in_back, tr, tl)
    scatter_gu = Scatter(p_gu, via_gu, in_gu, wr, wl)
    scatter_dn = Scatter(p_dn, via_dn, in_dn, wr, wl)
    home_out = Exchange(out_send, out_home)
    home_back = Exchange(back_send, back_home)

    pl.semaphore_wait(barrier, 4 + n_exp - 1)
    for load, gather in ((0, gather_wg), (4, gather_wu), (5, gather_wd)):
        loads[load].wait()
        gather.start()

    loads[1].wait()
    loads[2].wait()
    lane = lax.broadcasted_iota(jnp.int32, (tok, rows), 1)
    expert_of, slot_of = lane // cap, lane % cap
    token = lax.broadcasted_iota(jnp.int32, (tok, tok), 0)
    other = lax.broadcasted_iota(jnp.int32, (tok, tok), 1)

    def column_of(row):
        return jnp.sum(jnp.where(token == other, row, 0.0), axis=1, keepdims=True)

    def row_of(column):
        return jnp.sum(jnp.where(token == other, column, 0.0), axis=0, keepdims=True)

    gates = [column_of(gp_ref[k : k + 1, :]) for k in range(2)]
    choices = ids_ref[...].astype(F32)
    chosen = expert_of.astype(F32)
    named = [column_of(choices[k : k + 1, :]) == chosen for k in range(2)]
    either = (named[0] | named[1]).astype(F32).astype(BF16)
    earlier = (other < token).astype(F32).astype(BF16)
    before = jnp.dot(earlier, either, preferred_element_type=F32)
    here = before == slot_of.astype(F32)
    pick = [(named[k] & here).astype(F32).astype(BF16) for k in range(2)]
    pick_any = pick[0] + pick[1]

    def cols(n):
        return pl.ds(pl.multiple_of(n * tile, tile), tile)

    def deal_tile(n, _):
        c = cols(n)
        sent = lax.dot_general(pick_any, tok_ref[:, c], ROWS_ROWS, preferred_element_type=F32)
        x_send[:, :, c] = sent.astype(BF16).reshape(n_exp, cap, tile)
        return 0

    loads[3].wait()
    lax.fori_loop(0, n_tiles, deal_tile, 0)
    deal_x.start()
    x_buf[0, me] = x_send[me]

    def deal_grad_tile(n, _):
        c = cols(n)
        cot = cot_ref[:, c].astype(F32)
        sent = sum(
            lax.dot_general(
                pick[k], (gates[k] * cot).astype(BF16), ROWS_ROWS,
                preferred_element_type=F32,
            )
            for k in range(2)
        )
        g_send[:, :, c] = sent.astype(BF16).reshape(n_exp, cap, tile)
        return 0

    loads[6].wait()
    lax.fori_loop(0, n_tiles, deal_grad_tile, 0)
    g_buf[0, me] = g_send[me]

    wg = [wg_buf.at[s] for s in range(RING)]
    wu = [wu_buf.at[s] for s in range(RING)]
    wd = [wd_buf.at[s] for s in range(RING)]

    gather_wg.relay()
    deal_g.start()
    gather_wu.relay()
    deal_x.finish()
    gather_x.start()
    gather_wd.relay()
    deal_g.finish()
    gather_x.relay()
    gather_g.start()

    def forward(i):
        x = x_buf[i].reshape(rows, d)
        for j in range(RING):
            w = jnp.concatenate([wg[j][...], wu[j][...]], axis=1)
            pre = jnp.dot(x, w, preferred_element_type=F32)
            g, u = pre[:, :hs], pre[:, hs:]
            s = 1.0 / (1.0 + jnp.exp(-g))
            gs = g * s
            c = slice(j * hs, (j + 1) * hs)
            h = (gs * u).astype(BF16)
            h_buf[i, :, c] = h
            a_buf[i, :, c] = u * s * (1.0 + g * (1.0 - s))
            b_buf[i, :, c] = gs
            ht_buf[c, pl.ds(pl.multiple_of(i * rows, rows), rows)] = h.T

    def backward(i):
        g = g_buf[i].reshape(rows, d)
        for j in range(0, RING, 2):
            w = jnp.concatenate([wd[j][...], wd[j + 1][...]], axis=0)
            dh = lax.dot_general(g, w, COLS_COLS, preferred_element_type=F32)
            for jj in range(2):
                c = slice((j + jj) * hs, (j + jj + 1) * hs)
                part = dh[:, jj * hs : (jj + 1) * hs]
                dp = jnp.concatenate([part * a_buf[i, :, c], part * b_buf[i, :, c]], axis=1)
                dp = dp.astype(BF16)
                dp_buf[i, :, (j + jj) * 2 * hs : (j + jj + 1) * 2 * hs] = dp
                dpt_buf[j + jj, :, pl.ds(pl.multiple_of(i * rows, rows), rows)] = dp.T

    def store_rows(part, own, slot, c, value):
        if slot == 0:
            own[:, c] = value
        else:
            n = value.shape[0] // 2
            part[slot - 1, 0, :, c] = value[:n].astype(BF16)
            part[slot - 1, 1, :, c] = value[n:].astype(BF16)

    def out_part(i):
        def one(n, _):
            c = cols(n)
            w = jnp.concatenate([wd[j][:, c] for j in range(RING)], axis=0)
            store_rows(p_out, own_out, i, c, jnp.dot(h_buf[i], w, preferred_element_type=F32))
            return 0

        lax.fori_loop(0, n_tiles, one, 0)

    def back_part(i):
        def one(n, _):
            c = cols(n)
            w = jnp.concatenate(
                [r[c, :] for j in range(RING) for r in (wg[j], wu[j])], axis=1
            )
            value = lax.dot_general(dp_buf[i], w, COLS_COLS, preferred_element_type=F32)
            store_rows(p_back, own_back, i, c, value)
            return 0

        lax.fori_loop(0, n_tiles, one, 0)

    def gate_up_part(j):
        def one(n, _):
            c = cols(n)
            x = x_buf[:, :, :, c].reshape(RING * rows, tile)
            store_rows(p_gu, own_gu, j, c, jnp.dot(dpt_buf[j], x, preferred_element_type=F32))
            return 0

        lax.fori_loop(0, n_tiles, one, 0)

    def down_parts():
        def one(n, _):
            c = cols(n)
            g = g_buf[:, :, :, c].reshape(RING * rows, tile)
            value = jnp.dot(ht_buf[...], g, preferred_element_type=F32)
            for j in range(RING):
                store_rows(p_dn, own_dn, j, c, value[j * hs : (j + 1) * hs])
            return 0

        lax.fori_loop(0, n_tiles, one, 0)

    def both_sides(body):
        def step(k, _):
            body(1 + 2 * k)
            return 0

        lax.fori_loop(0, 2, step, 0)

    def total(arrived, own, sent):
        for h in range(2):
            value = (
                own[h * half : (h + 1) * half, :]
                + arrived[0, h].astype(F32)
                + arrived[1, h].astype(F32)
            )
            sent[h * experts_half : (h + 1) * experts_half] = value.astype(BF16).reshape(
                experts_half, cap, d
            )

    for gather in (gather_wg, gather_wu):
        gather.sides()
        gather.finish()
    forward(0)
    gather_x.sides()
    both_sides(forward)
    gather_x.finish()
    forward(2)
    gather_g.relay()
    gather_wd.sides()
    gather_wd.finish()
    out_part(2)
    scatter_out.far()
    out_part(1)
    out_part(3)
    scatter_out.near()
    out_part(0)

    backward(0)
    gather_g.sides()
    both_sides(backward)
    scatter_out.add()
    gather_g.finish()
    backward(2)
    back_part(2)
    scatter_back.far()
    back_part(1)
    back_part(3)
    scatter_back.near()
    scatter_out.finish()
    total(in_out, own_out, out_send)
    home_out.start()
    out_home[me] = out_send[me]
    gate_up_part(2)
    scatter_back.add()
    scatter_gu.far()
    gate_up_part(1)
    gate_up_part(3)
    scatter_gu.near()
    down_parts()
    scatter_dn.far()
    scatter_dn.near()
    back_part(0)
    scatter_gu.add()
    scatter_back.finish()
    total(in_back, own_back, back_send)
    home_back.start()
    back_home[me] = back_send[me]
    gate_up_part(0)

    home_out.finish()

    def mix_tile(n, inner):
        c = cols(n)
        home = out_home[:, :, c].reshape(rows, tile)
        per = [jnp.dot(pick[k], home, preferred_element_type=F32) for k in range(2)]
        mixed_ref[:, c] = (gates[0] * per[0] + gates[1] * per[1]).astype(BF16)
        cot = cot_ref[:, c].astype(F32)
        return tuple(
            inner[k] + jnp.sum(cot * per[k], axis=1, keepdims=True) for k in range(2)
        )

    zero = jnp.zeros((tok, 1), F32)
    inner = lax.fori_loop(0, n_tiles, mix_tile, (zero, zero))
    for k in range(2):
        dgate_ref[k : k + 1, :] = row_of(inner[k])

    scatter_dn.add()
    home_back.finish()

    def home_tile(n, _):
        c = cols(n)
        home = back_home[:, :, c].reshape(rows, tile)
        dtok_ref[:, c] = jnp.dot(pick_any, home, preferred_element_type=F32).astype(BF16)
        return 0

    lax.fori_loop(0, n_tiles, home_tile, 0)

    scatter_gu.finish()
    for h, ref in enumerate((dwg_ref, dwu_ref)):
        value = (
            own_gu[h * hs : (h + 1) * hs, :]
            + in_gu[0, h].astype(F32)
            + in_gu[1, h].astype(F32)
        )
        ref[...] = value.T

    scatter_dn.finish()
    for h in range(2):
        r = slice(h * hs // 2, (h + 1) * hs // 2)
        dwd_ref[r, :] = own_dn[r, :] + in_dn[0, h].astype(F32) + in_dn[1, h].astype(F32)

    for flow in flows:
        flow.sent()


def write_kernel(*refs):
    n = len(refs) // 2
    sem = refs[-1]
    copies = [pltpu.make_async_copy(refs[k], refs[n + k], sem.at[k]) for k in range(n)]
    for c in copies:
        c.start()
    for c in copies:
        c.wait()


def per_device(tokens, gate_probs, expert_ids, cotangent, gate_weight, up_weight, down_weight):
    tok, d = tokens.shape
    n_exp = lax.axis_size("expert")
    cap = 2 * tok // n_exp
    rows = 2 * tok
    hs = gate_weight.shape[2]
    hidden = RING * hs
    n_out, n_in = 5 + 4 + 4, 4 * 5 + 3 * 4 + 4
    vmem = pltpu.VMEM
    shapes = [
        vmem((tok, d), BF16),
        vmem((tok, d), BF16),
        vmem((2, tok), F32),
        vmem((2, tok), jnp.int32),
        vmem((RING, n_exp, cap, d), BF16),
        vmem((RING, n_exp, cap, d), BF16),
        vmem((RING, d, hs), BF16),
        vmem((RING, d, hs), BF16),
        vmem((RING, hs, d), BF16),
        vmem((n_exp, cap, d), BF16),
        vmem((n_exp, cap, d), BF16),
        vmem((RING, rows, hidden), F32),
        vmem((RING, rows, hidden), F32),
        vmem((RING, rows, hidden), BF16),
        vmem((hidden, RING * rows), BF16),
        vmem((RING, rows, 2 * hidden), BF16),
        vmem((RING, 2 * hs, RING * rows), BF16),
    ]
    heights = (rows, rows, 2 * hs, hs)
    shapes += [vmem((3, 2, n // 2, d), BF16) for n in heights]
    shapes += [vmem((2, n // 2, d), BF16) for n in heights]
    shapes += [vmem((2, 2, n // 2, d), BF16) for n in heights]
    shapes += [vmem((n, d), F32) for n in heights]
    shapes += [vmem((n_exp, cap, d), BF16) for _ in range(4)]
    shapes += [pltpu.SemaphoreType.DMA((n,)) for n in (n_out, n_in, 7)]
    here, away = pl.BlockSpec(memory_space=pltpu.VMEM), pl.BlockSpec(memory_space=pl.ANY)
    results = [
        ((tok, d), BF16), ((tok, d), BF16), ((2, tok), F32),
        ((d, hs), F32), ((d, hs), F32), ((hs, d), F32),
    ]
    inside = pl.pallas_call(
        functools.partial(layer_kernel, n_exp),
        out_shape=[pltpu.VMEM(*r) for r in results],
        in_specs=[away] * 7,
        out_specs=[here] * len(results),
        scratch_shapes=shapes,
        compiler_params=pltpu.CompilerParams(
            collective_id=0, has_side_effects=True, vmem_limit_bytes=58 * 1024 * 1024
        ),
    )(
        tokens, gate_probs.T, expert_ids.T, cotangent,
        gate_weight[0], up_weight[0], down_weight[0],
    )
    mixed, d_tokens, d_gates, d_gate_w, d_up_w, d_down = pl.pallas_call(
        write_kernel,
        out_shape=[jax.ShapeDtypeStruct(*r) for r in results],
        in_specs=[here] * len(results),
        out_specs=[away] * len(results),
        scratch_shapes=[pltpu.SemaphoreType.DMA((len(results),))],
        compiler_params=pltpu.CompilerParams(vmem_limit_bytes=1024 * 1024),
    )(*inside)
    return mixed, d_tokens, d_gates.T, d_gate_w[None], d_up_w[None], d_down[None]


def solution(mesh):
    rows = P(("expert", "fsdp"), None)
    hidden = P("expert", None, "fsdp")
    hidden_rows = P("expert", "fsdp", None)
    return jax.shard_map(
        per_device,
        mesh=mesh,
        in_specs=(rows, rows, rows, rows, hidden, hidden, hidden_rows),
        out_specs=(rows, rows, rows, hidden, hidden, hidden_rows),
        check_vma=False,
    )
```
